512 devices in a mesh: lat: 32 (over x_hi, z, core), lon: 16 (over y, x_lo).
Axes of the slice: x: 4 (x_hi: 2, x_lo: 2; x = x_hi * 2 + x_lo), y: 8, z: 8, core: 2. Of those that a mesh axis runs over, the one named last changes fastest.
Arguments:
- nodes: bfloat16 [32, 16, 128, 512], P('lat', 'lon'), may hold values from -6 to 6
- top_nodes: bfloat16 [1024, 512], P('lat'), may hold values from -6 to 6
- cotangent: bfloat16 [32, 16, 128, 512], P('lat', 'lon'), may hold values from -3 to 3
- w_src: bfloat16 [512, 512], replicated, may hold values from -0.25 to 0.25
- w_dst: bfloat16 [512, 512], replicated, may hold values from -0.25 to 0.25
- w_msg: bfloat16 [512, 512], replicated, may hold values from -0.25 to 0.25
- w_top: bfloat16 [512, 512], replicated, may hold values from -0.25 to 0.25
- src_code: int32 [32, 16, 1024], P('lat', 'lon'), may hold values from 0 to 8
- src_node: int32 [32, 16, 1024], P('lat', 'lon'), may hold values from 0 to 127
- dst_node: int32 [32, 16, 1024], P('lat', 'lon'), may hold values from 0 to 127
- edge_count: int32 [32, 16], P('lat', 'lon'), may hold values from 256 to 1024, as said below
- parent: int32 [32, 16, 128], P('lat', 'lon'), may hold values from 0 to 1023, as said below
Outputs:
- updated: bfloat16 [32, 16, 128, 512], P('lat', 'lon')
- weight_grads: bfloat16 [4, 512, 512], replicated
- d_top: bfloat16 [1024, 512], P(('lat', 'lon'))
The draws below stay inside these ranges and needn't reach their ends.
Inputs may be any that keep to these rules, and one draw needn't show every extreme that they name: `edge_count`: some block has all 1024 slots live. Top-level nodes come in bands of 32, one band for the one block row. Node n of block (i, j) lies at longitude position p = j * 128 + n, and c = p * 32 // 2048 is the band column above it. Its parent is (i) * 32 + k for a column k of 0 to 31 with |k - c| <= 2.
All inputs are finite; a program needn't handle non-finite values.
Results may differ from the reference program's by a relative error of at most 0.006.
Values may be sent and summed in bfloat16 or wider, within the bound.
No kernel may reach another device: no remote copies, remote signals or barrier semaphores. Data moves between devices by JAX's collectives and lax.ppermute only.
A program may use at most 64 MiB of HBM per device.

```python
import math
import jax
import jax.numpy as jnp
from jax import lax

D = 512
BLOCK = 128
E_BLK = 1024
BI_DEV = 1
BJ_DEV = 1
TOP_DEV = 32
NBI = 32
NBJ = 16
TOP = 1024


def draw_edge_count(key, part):
    first_key, second_key = jax.random.split(key)
    counts = jax.random.randint(first_key, (NBI, NBJ), E_BLK // 4, E_BLK + 1)
    chosen = jax.random.randint(second_key, (), 0, NBI * NBJ)
    flat_ids = jnp.arange(NBI * NBJ).reshape(NBI, NBJ)
    return jnp.where(flat_ids == chosen, E_BLK, counts).astype(jnp.int32)


def draw_parent(key, part):
    reach = TOP_DEV * BJ_DEV // NBJ
    block_row = jnp.arange(NBI, dtype=jnp.int32)[:, None, None]
    position = jnp.arange(NBJ, dtype=jnp.int32)[None, :, None] * BLOCK + jnp.arange(BLOCK, dtype=jnp.int32)[None, None, :]
    centre = position * TOP_DEV // (NBJ * BLOCK)
    offset = jax.random.randint(jax.random.fold_in(key, 17), (NBI, NBJ, BLOCK), -reach, reach + 1)
    column = jnp.clip(centre + offset, 0, TOP_DEV - 1)
    return (block_row // BI_DEV * TOP_DEV + column).astype(jnp.int32)


def place_ends(array, stream_key, smallest, top_value):
    extent = array.shape
    spot = [jax.random.randint(jax.random.fold_in(stream_key, axis), (), 0, extent[axis]) for axis in range(len(extent))]
    array = array.at[tuple(spot)].set(smallest)
    longest = extent.index(max(extent))
    spot[longest] = (spot[longest] + 1) % extent[longest]
    return array.at[tuple(spot)].set(top_value)


def block_scale(stream_key, dims, cuts, low, top_value):
    loudness = 1.0
    for axis_at, blocks in cuts:
        draws = jax.random.uniform(jax.random.fold_in(jax.random.fold_in(stream_key, 6), axis_at), (blocks,), jnp.float32, low / len(cuts), top_value / len(cuts))
        loudness = loudness * jnp.repeat(jnp.exp(draws), dims[axis_at] // blocks).reshape((-1,) + (1,) * (len(dims) - 1 - axis_at))
    return loudness


def noise(own_key, shape, deviation, most, shards=(), held_as=jnp.bfloat16):
    values = deviation * jax.random.normal(own_key, shape, jnp.float32)
    if shards:
        values = values * block_scale(own_key, shape, shards, -0.22, 0.18)
    return jnp.clip(values, -most, most).astype(held_as)


def setup_inputs(seed: int = 0) -> dict:
    splits = jax.random.split(jax.random.key(seed), 13)
    return {
        "nodes": noise(splits[0], (NBI, NBJ, BLOCK, D), 1.0, 6.0, ((0, 32), (1, 16))),
        "top_nodes": noise(splits[1], (TOP, D), 1.0, 6.0, ((0, 32),)),
        "cotangent": noise(splits[2], (NBI, NBJ, BLOCK, D), 0.5, 3.0, ((0, 32), (1, 16))),
        "w_src": noise(splits[3], (D, D), D ** -0.5, 0.25),
        "w_dst": noise(splits[4], (D, D), D ** -0.5, 0.25),
        "w_msg": noise(splits[5], (D, D), D ** -0.5, 0.25),
        "w_top": noise(splits[6], (D, D), D ** -0.5, 0.25),
        "src_code": place_ends(jax.random.randint(splits[7], (NBI, NBJ, E_BLK), 0, 9), jax.random.fold_in(splits[7], 1), 0, 8).astype(jnp.int32),
        "src_node": place_ends(jax.random.randint(splits[8], (NBI, NBJ, E_BLK), 0, BLOCK), jax.random.fold_in(splits[8], 1), 0, BLOCK - 1).astype(jnp.int32),
        "dst_node": place_ends(jax.random.randint(splits[9], (NBI, NBJ, E_BLK), 0, BLOCK), jax.random.fold_in(splits[9], 1), 0, BLOCK - 1).astype(jnp.int32),
        "edge_count": draw_edge_count(jax.random.fold_in(splits[12], 71), 0),
        "parent": draw_parent(jax.random.fold_in(splits[12], 71), 0),
    }


def silu_slope(values):
    sigmoid_v = jax.nn.sigmoid(values)
    return sigmoid_v * (1.0 + values * (1.0 - sigmoid_v))

def reference(nodes, top_nodes, cotangent, w_src, w_dst, w_msg, w_top, src_code, src_node, dst_node, edge_count, parent):
    block_rows, block_cols, block_size, features = nodes.shape
    top_count = top_nodes.shape[0]
    slot_count = src_code.shape[-1]
    ext_cols = block_cols + 2
    top_table = jnp.dot(top_nodes, w_top, preferred_element_type=jnp.float32).astype(jnp.bfloat16)
    padded = jnp.pad(nodes, ((1, 1), (1, 1), (0, 0), (0, 0)))
    col_ids = jnp.arange(block_cols, dtype=jnp.int32)[:, None]
    slot_ids = jnp.arange(slot_count, dtype=jnp.int32)
    row_nodes = block_cols * block_size

    def row_step(carry, inputs):
        grad_src, grad_dst, grad_msg, table_sum = carry
        row_id, row_feat, row_cot, code, snode, dnode, counts, parents = inputs
        three_rows = lax.dynamic_slice_in_dim(padded, row_id, 3, 0).reshape(-1, features)
        src_proj = jnp.dot(three_rows, w_src, preferred_element_type=jnp.float32)
        local_rows = row_feat.reshape(-1, features)
        dst_proj = jnp.dot(local_rows, w_dst, preferred_element_type=jnp.float32)
        src_idx = ((code // 3 * ext_cols + col_ids + code % 3) * block_size + snode).reshape(-1).astype(jnp.int32)
        dst_idx = (col_ids * block_size + dnode).reshape(-1).astype(jnp.int32)
        live = (slot_ids[None, :] < counts[:, None]).astype(jnp.float32).reshape(-1, 1)
        pre_act = src_proj[src_idx] + dst_proj[dst_idx]
        hidden = jax.nn.silu(pre_act).astype(jnp.bfloat16)
        msg_pre = jnp.dot(hidden, w_msg, preferred_element_type=jnp.float32)
        message = (jax.nn.silu(msg_pre) * live).astype(jnp.bfloat16)
        inflow = jax.ops.segment_sum(message.astype(jnp.float32), dst_idx, num_segments=row_nodes)
        parent_ids = parents.reshape(-1).astype(jnp.int32)
        node_pre = inflow + top_table[parent_ids].astype(jnp.float32)
        updated = (local_rows.astype(jnp.float32) + jax.nn.silu(node_pre)).astype(jnp.bfloat16)
        node_grad = (row_cot.reshape(-1, features).astype(jnp.float32) * silu_slope(node_pre)).astype(jnp.bfloat16)
        table_sum = table_sum + jax.ops.segment_sum(node_grad.astype(jnp.float32), parent_ids, num_segments=top_count)
        msg_grad = node_grad[dst_idx].astype(jnp.float32) * live
        pre_grad = (msg_grad * silu_slope(msg_pre)).astype(jnp.bfloat16)
        grad_msg = grad_msg + jnp.dot(hidden.T, pre_grad, preferred_element_type=jnp.float32)
        hidden_grad = jnp.dot(pre_grad, w_msg.T, preferred_element_type=jnp.float32)
        act_grad = (hidden_grad * silu_slope(pre_act)).astype(jnp.bfloat16)
        dst_grad = jax.ops.segment_sum(act_grad.astype(jnp.float32), dst_idx, num_segments=row_nodes).astype(jnp.bfloat16)
        grad_dst = grad_dst + jnp.dot(local_rows.T, dst_grad, preferred_element_type=jnp.float32)
        grad_src = grad_src + jnp.dot(three_rows[src_idx].T, act_grad, preferred_element_type=jnp.float32)
        return ((grad_src, grad_dst, grad_msg, table_sum), updated.reshape(block_cols, block_size, features))
    zero_square = jnp.zeros((features, features), jnp.float32)
    init = (zero_square, zero_square, zero_square, jnp.zeros((top_count, features), jnp.float32))
    inputs = (jnp.arange(block_rows, dtype=jnp.int32), nodes, cotangent, src_code, src_node, dst_node, edge_count, parent)
    carry, updated = lax.scan(row_step, init, inputs)
    grad_src, grad_dst, grad_msg, table_sum = carry
    table_grad = table_sum.astype(jnp.bfloat16)
    d_top = jnp.dot(table_grad, w_top.T, preferred_element_type=jnp.float32).astype(jnp.bfloat16)
    grad_top = jnp.dot(top_nodes.T, table_grad, preferred_element_type=jnp.float32)
    grad_scale = 8.0 / math.sqrt(block_rows * block_cols * block_size)
    weight_grads = (jnp.stack([grad_src, grad_dst, grad_msg, grad_top]) * grad_scale).astype(jnp.bfloat16)
    return (updated, weight_grads, d_top)
```

```python
import math

import jax
import jax.numpy as jnp
from jax import lax
from jax.sharding import Mesh
from jax.sharding import PartitionSpec as P

LAT = ("x_hi", "z_hi", "z_lo", "core")
LON = ("y_hi", "y_lo", "x_lo")


def extended_2(block, sides, width):
    for axis, dim in sides:
        count = lax.axis_size(axis)
        forward = [(i, i + 1) for i in range(count - 1)]
        backward = [(target, source) for source, target in forward]
        low = lax.ppermute(
            lax.slice_in_dim(block, block.shape[dim] - width, None, axis=dim), axis, forward
        )
        high = lax.ppermute(lax.slice_in_dim(block, 0, width, axis=dim), axis, backward)
        block = jnp.concatenate([low, block, high], axis=dim)
    return block


def silu_slope(values):
    sigmoid_v = jax.nn.sigmoid(values)
    return sigmoid_v * (1.0 + values * (1.0 - sigmoid_v))


def contract_rows(left_mat, right_mat):
    return lax.dot_general(
        left_mat, right_mat, (((0,), (0,)), ((), ())), preferred_element_type=jnp.float32
    )


NEAR = ("x_hi", "z_lo", "y_lo", "x_lo")
FAR = ("z_hi", "y_hi")


def all_sum(stack, scale):
    part = stack.astype(jnp.bfloat16)
    for axes in (("core",), NEAR, FAR):
        count = lax.axis_size(axes)
        part = lax.all_to_all(part, axes, 0, 0, tiled=True)
        part = jnp.sum(
            part.reshape(count, -1, part.shape[-1]).astype(jnp.float32), axis=0
        )
        if axes != FAR:
            part = part.astype(jnp.bfloat16)
    part = (part * scale).astype(jnp.bfloat16)
    for axes in (FAR, NEAR, ("core",)):
        count = lax.axis_size(axes)
        copies = jnp.broadcast_to(part[None], (count,) + part.shape).reshape(-1, part.shape[-1])
        part = lax.all_to_all(copies, axes, 0, 0, tiled=True)
    return part


def shards(
    nodes,
    top_nodes,
    cotangent,
    w_src,
    w_dst,
    w_msg,
    w_top,
    src_code,
    src_node,
    dst_node,
    edge_count,
    parent,
):
    block_rows, block_cols, block_size, features = nodes.shape
    block_count = block_rows * block_cols
    slot_count = src_code.shape[-1]
    ext_cols = block_cols + 2
    top_local = top_nodes.shape[0]
    owner_rows = top_local // lax.axis_size(LON)
    lon_index = lax.axis_index(LON)
    band_start = lax.axis_index(LAT) * top_local
    parents = parent.reshape(-1)
    band_ids = parents - band_start
    window_ids = band_ids - (lon_index - 1) * owner_rows
    top_table = jnp.dot(top_nodes, w_top, preferred_element_type=jnp.float32).astype(jnp.bfloat16)
    table_rows = jnp.take(top_table, band_ids, axis=0)
    extended = extended_2(nodes, ((LAT, 0), (LON, 1)), 1)
    ext_flat = extended.reshape(-1, features)
    src_proj = jnp.dot(ext_flat, w_src, preferred_element_type=jnp.float32)
    local_rows = nodes.reshape(-1, features)
    dst_proj = jnp.dot(local_rows, w_dst, preferred_element_type=jnp.float32)
    block_row = lax.iota(jnp.int32, block_rows)[:, None, None]
    block_col = lax.iota(jnp.int32, block_cols)[None, :, None]
    src_idx = (
        ((block_row + src_code // 3) * ext_cols + block_col + src_code % 3) * block_size + src_node
    ).reshape(-1)
    dst_idx = ((block_row * block_cols + block_col) * block_size + dst_node).reshape(-1)
    live_slot = lax.iota(jnp.int32, slot_count)[None, None, :] < edge_count[:, :, None]
    node_ids = lax.iota(jnp.int32, block_size)[None, :, None]
    one_hot = ((dst_node == node_ids) & live_slot).astype(jnp.bfloat16)
    pre_act = jnp.take(src_proj, src_idx, axis=0) + jnp.take(dst_proj, dst_idx, axis=0)
    hidden = jax.nn.silu(pre_act).astype(jnp.bfloat16)
    msg_pre = jnp.dot(hidden, w_msg, preferred_element_type=jnp.float32)
    message = jax.nn.silu(msg_pre).astype(jnp.bfloat16)
    inflow = jnp.einsum(
        "bne,bed->bnd",
        one_hot,
        message.reshape(block_count, slot_count, features),
        preferred_element_type=jnp.float32,
    ).reshape(-1, features)
    node_pre = inflow + table_rows.astype(jnp.float32)
    updated = (
        (local_rows.astype(jnp.float32) + jax.nn.silu(node_pre))
        .astype(jnp.bfloat16)
        .reshape(nodes.shape)
    )
    node_grad = (cotangent.reshape(-1, features).astype(jnp.float32) * silu_slope(node_pre)).astype(
        jnp.bfloat16
    )
    msg_grad = jnp.einsum(
        "bne,bnd->bed",
        one_hot,
        node_grad.reshape(block_count, block_size, features),
        preferred_element_type=jnp.float32,
    ).reshape(-1, features)
    pre_grad = (msg_grad * silu_slope(msg_pre)).astype(jnp.bfloat16)
    grad_msg = contract_rows(hidden, pre_grad)
    hidden_grad = lax.dot_general(
        pre_grad, w_msg, (((1,), (1,)), ((), ())), preferred_element_type=jnp.float32
    )
    act_grad = (hidden_grad * silu_slope(pre_act)).astype(jnp.bfloat16)
    dst_grad = (
        jnp.einsum(
            "bne,bed->bnd",
            one_hot,
            act_grad.reshape(block_count, slot_count, features),
            preferred_element_type=jnp.float32,
        )
        .astype(jnp.bfloat16)
        .reshape(-1, features)
    )
    grad_dst = contract_rows(local_rows, dst_grad)
    grad_src = contract_rows(jnp.take(ext_flat, src_idx, axis=0), act_grad)
    window_cols = lax.iota(jnp.int32, 3 * owner_rows)
    picks = (window_ids[:, None] == window_cols[None, :]).astype(jnp.bfloat16)
    window_sum = contract_rows(picks, node_grad)
    rims = jnp.concatenate([window_sum[:owner_rows], window_sum[2 * owner_rows :]], axis=0)
    rim_parts = extended_2(rims, ((LON, 0),), owner_rows)
    table_sum = (
        window_sum[owner_rows : 2 * owner_rows]
        + rim_parts[:owner_rows]
        + rim_parts[3 * owner_rows :]
    )
    table_grad = table_sum.astype(jnp.bfloat16)
    top_mine = lax.dynamic_slice_in_dim(top_nodes, lon_index * owner_rows, owner_rows, 0)
    d_top = lax.dot_general(
        table_grad, w_top, (((1,), (1,)), ((), ())), preferred_element_type=jnp.float32
    ).astype(jnp.bfloat16)
    grad_top = contract_rows(top_mine, table_grad)
    nodes_total = block_count * block_size * lax.axis_size(LAT) * lax.axis_size(LON)
    grad_scale = 8.0 / math.sqrt(nodes_total)
    stack = jnp.stack([grad_src, grad_dst, grad_msg, grad_top])
    lanes = 128
    tiles = features // lanes
    by_lane_tile = stack.reshape(4 * features, tiles, lanes).transpose(1, 0, 2).reshape(-1, lanes)
    summed = all_sum(by_lane_tile, grad_scale)
    weight_grads = (
        summed.reshape(tiles, 4, features, lanes).transpose(1, 2, 0, 3).reshape(4, features, features)
    )
    return (updated, weight_grads, d_top)


def solution(mesh):
    fine = Mesh(
        mesh.devices.reshape(2, 4, 2, 2, 4, 2, 2),
        ("x_hi", "z_hi", "z_lo", "core", "y_hi", "y_lo", "x_lo"),
    )
    placed = (
        P(LAT, LON, None, None),
        P(LAT, None),
        P(LAT, LON, None, None),
        P(),
        P(),
        P(),
        P(),
        P(LAT, LON, None),
        P(LAT, LON, None),
        P(LAT, LON, None),
        P(LAT, LON),
        P(LAT, LON, None),
    )
    return jax.shard_map(
        shards,
        mesh=fine,
        in_specs=placed,
        out_specs=(P(LAT, LON, None, None), P(), P(LAT + LON, None)),
        check_vma=False,
    )
```

```python
import math

import jax
import jax.numpy as jnp
from jax import lax
from jax.experimental import pallas as pl
from jax.experimental.pallas import tpu as pltpu
from jax.sharding import Mesh
from jax.sharding import PartitionSpec as P

LAT = ("x_hi", "z_hi", "z_lo", "core")
LON = ("y_hi", "y_lo", "x_lo")
NEAR = ("x_hi", "z_lo", "y_lo", "x_lo")
FAR = ("z_hi", "y_hi")
CORE = ("core",)
LANES = 128
CHUNK = 256
BF16 = jnp.bfloat16
F32 = jnp.float32


def exchange(part, axes):
    return lax.all_to_all(part, axes, 0, 0, tiled=True)


def reduce_stage(part, axes):
    got = exchange(part, axes)
    count = lax.axis_size(axes)
    return jnp.sum(got.reshape(count, -1, got.shape[-1]).astype(F32), axis=0)


def gather_stage(part, axes):
    count = lax.axis_size(axes)
    copies = jnp.broadcast_to(part[None], (count,) + part.shape)
    return exchange(copies.reshape(-1, part.shape[-1]), axes)


def all_sum(part, scale):
    features = part.shape[-1]
    tiles = features // LANES
    part = reduce_stage(part, CORE).astype(BF16)
    part = reduce_stage(part, NEAR).astype(BF16)
    rows = part.shape[0]
    part = part.reshape(rows, tiles, LANES).transpose(1, 0, 2).reshape(-1, LANES)
    part = (reduce_stage(part, FAR) * scale).astype(BF16)
    part = gather_stage(part, FAR)
    part = part.reshape(tiles, rows, LANES).transpose(1, 0, 2).reshape(rows, features)
    part = gather_stage(part, NEAR)
    return gather_stage(part, CORE)


def both_ways(block, axis):
    count = lax.axis_size(axis)
    forward = [(i, i + 1) for i in range(count - 1)]
    backward = [(target, source) for source, target in forward]
    return lax.ppermute(block, axis, forward), lax.ppermute(block, axis, backward)


def silu_parts(values):
    sigmoid_v = jax.nn.sigmoid(values)
    return values * sigmoid_v, sigmoid_v * (1.0 + values * (1.0 - sigmoid_v))


def mm(left, right):
    return lax.dot_general(left, right, (((1,), (0,)), ((), ())), preferred_element_type=F32)


def mm_rows(left, right):
    return lax.dot_general(left, right, (((0,), (0,)), ((), ())), preferred_element_type=F32)


def mm_cols(left, right):
    return lax.dot_general(left, right, (((1,), (1,)), ((), ())), preferred_element_type=F32)


def column(row):
    return jnp.transpose(jnp.broadcast_to(row, (8, row.shape[-1])))[:, :1]


def one_hot_cols(ids_column, width):
    lane_ids = lax.broadcasted_iota(jnp.int32, (ids_column.shape[0], width), 1)
    return (ids_column == lane_ids).astype(F32).astype(BF16)


def one_hot_rows(ids_row, height):
    row_ids = lax.broadcasted_iota(jnp.int32, (height, ids_row.shape[-1]), 0)
    return (ids_row == row_ids).astype(F32).astype(BF16)


def block_kernel(
    low_ref,
    mid_ref,
    high_ref,
    nodes_ref,
    top_ref,
    cot_ref,
    w_src_ref,
    w_dst_ref,
    w_msg_ref,
    w_top_ref,
    src_ref,
    dst_ref,
    band_ref,
    updated_ref,
    grads_ref,
    window_ref,
    ext,
    picked,
    hidden,
    pre_grad,
    act_grad,
    act_slope,
    msg_slope,
    dst_cols,
):
    slots = src_ref.shape[-1]
    block, features = nodes_ref.shape
    third = low_ref.shape[0]
    ext[0:third, :] = low_ref[...]
    ext[third : 2 * third, :] = mid_ref[...]
    ext[2 * third :, :] = high_ref[...]
    nodes = nodes_ref[...]
    src_col = column(src_ref[...])
    dst_col = column(dst_ref[...])
    dst_rows = one_hot_rows(dst_ref[...], block)
    inflow = jnp.zeros((block, features), F32)
    for start in range(0, slots, CHUNK):
        span = slice(start, start + CHUNK)
        gathered = mm(one_hot_cols(src_col[span], ext.shape[0]), ext[...]).astype(BF16)
        picked[span, :] = gathered
        at_dst = one_hot_cols(dst_col[span], block)
        dst_cols[span, :] = at_dst
        local = mm(at_dst, nodes).astype(BF16)
        pre_act = mm(gathered, w_src_ref[...]) + mm(local, w_dst_ref[...])
        value, slope = silu_parts(pre_act)
        act_slope[span, :] = slope
        hid = value.astype(BF16)
        hidden[span, :] = hid
        value, slope = silu_parts(mm(hid, w_msg_ref[...]))
        msg_slope[span, :] = slope
        inflow = inflow + mm(dst_rows[:, span], value.astype(BF16))
    top_count = top_ref.shape[0]
    top_nodes = top_ref[...]
    top_table = mm(top_nodes, w_top_ref[...]).astype(BF16)
    band_col = column(band_ref[...])
    node_pre = inflow + mm(one_hot_cols(band_col, top_count), top_table)
    value, slope = silu_parts(node_pre)
    updated_ref[...] = (nodes.astype(F32) + value).astype(BF16)
    node_grad = (cot_ref[...].astype(F32) * slope).astype(BF16)
    window = mm(one_hot_rows(band_ref[...], top_count), node_grad)
    window_ref[...] = window
    grads_ref[3] = mm_rows(top_nodes, window.astype(BF16)).astype(BF16)
    dst_grad = jnp.zeros((block, features), F32)
    for start in range(0, slots, CHUNK):
        span = slice(start, start + CHUNK)
        msg_grad = mm(dst_cols[span, :], node_grad)
        grad = (msg_grad * msg_slope[span, :]).astype(BF16)
        pre_grad[span, :] = grad
        grad = (mm_cols(grad, w_msg_ref[...]) * act_slope[span, :]).astype(BF16)
        act_grad[span, :] = grad
        dst_grad = dst_grad + mm(dst_rows[:, span], grad)
    grads_ref[0] = mm_rows(picked[...], act_grad[...]).astype(BF16)
    grads_ref[1] = mm_rows(nodes, dst_grad.astype(BF16)).astype(BF16)
    grads_ref[2] = mm_rows(hidden[...], pre_grad[...]).astype(BF16)


def block_round(*args):
    nodes, top_nodes = args[3], args[4]
    slots = args[10].shape[-1]
    block, features = nodes.shape
    ext_rows = 3 * args[0].shape[0]
    return pl.pallas_call(
        block_kernel,
        out_shape=(
            jax.ShapeDtypeStruct((block, features), BF16),
            jax.ShapeDtypeStruct((4, features, features), BF16),
            jax.ShapeDtypeStruct((top_nodes.shape[0], features), F32),
        ),
        scratch_shapes=[
            pltpu.VMEM((ext_rows, features), BF16),
            pltpu.VMEM((slots, features), BF16),
            pltpu.VMEM((slots, features), BF16),
            pltpu.VMEM((slots, features), BF16),
            pltpu.VMEM((slots, features), BF16),
            pltpu.VMEM((slots, features), F32),
            pltpu.VMEM((slots, features), F32),
            pltpu.VMEM((slots, block), BF16),
        ],
        compiler_params=pltpu.CompilerParams(vmem_limit_bytes=48 << 20),
        name="block_round",
    )(*args)


def shards(
    nodes,
    top_nodes,
    cotangent,
    w_src,
    w_dst,
    w_msg,
    w_top,
    src_code,
    src_node,
    dst_node,
    edge_count,
    parent,
):
    block_size, features = nodes.shape[2:]
    slots = src_code.shape[-1]
    top_local = top_nodes.shape[0]
    owner_rows = top_local // lax.axis_size(LON)
    lon_index = lax.axis_index(LON)
    band_start = lax.axis_index(LAT) * top_local
    own = nodes.reshape(block_size, features)
    west, east = both_ways(own, LON)
    mid = jnp.concatenate([west, own, east], axis=0)
    low, high = both_ways(mid, LAT)
    src_idx = (src_code * block_size + src_node).reshape(1, slots)
    live_slot = lax.broadcasted_iota(jnp.int32, (1, slots), 1) < edge_count
    dst_idx = jnp.where(live_slot, dst_node.reshape(1, slots), block_size)
    band_ids = parent.reshape(1, block_size) - band_start
    updated, grads, window = block_round(
        low,
        mid,
        high,
        own,
        top_nodes,
        cotangent.reshape(block_size, features),
        w_src,
        w_dst,
        w_msg,
        w_top,
        src_idx,
        dst_idx,
        band_ids,
    )
    nodes_total = block_size * lax.axis_size(LAT) * lax.axis_size(LON)
    grad_scale = 8.0 / math.sqrt(nodes_total)
    weight_grads = all_sum(grads.reshape(-1, features), grad_scale)
    padded = jnp.pad(window, ((owner_rows, owner_rows), (0, 0)))
    triple = lax.dynamic_slice_in_dim(padded, lon_index * owner_rows, 3 * owner_rows, 0)
    count = lax.axis_size(LON)
    forward = [(i, i + 1) for i in range(count - 1)]
    backward = [(target, source) for source, target in forward]
    from_left = lax.ppermute(triple[2 * owner_rows :], LON, forward)
    from_right = lax.ppermute(triple[:owner_rows], LON, backward)
    table_grad = (triple[owner_rows : 2 * owner_rows] + from_left + from_right).astype(BF16)
    d_top = lax.dot_general(
        table_grad, w_top, (((1,), (1,)), ((), ())), preferred_element_type=F32
    ).astype(BF16)
    return (
        updated.reshape(nodes.shape),
        weight_grads.reshape(4, features, features),
        d_top,
    )


def solution(mesh):
    lat_count, lon_count = mesh.shape["lat"], mesh.shape["lon"]
    fine = Mesh(
        mesh.devices.reshape(2, lat_count // 8, 2, 2, lon_count // 4, 2, 2),
        LAT + LON,
    )
    placed = (
        P(LAT, LON, None, None),
        P(LAT, None),
        P(LAT, LON, None, None),
        P(),
        P(),
        P(),
        P(),
        P(LAT, LON, None),
        P(LAT, LON, None),
        P(LAT, LON, None),
        P(LAT, LON),
        P(LAT, LON, None),
    )
    return jax.shard_map(
        shards,
        mesh=fine,
        in_specs=placed,
        out_specs=(P(LAT, LON, None, None), P(), P(LAT + LON, None)),
        check_vma=False,
    )
```

```python
import math

import jax
import jax.numpy as jnp
from jax import lax
from jax.experimental import pallas as pl
from jax.experimental.pallas import tpu as pltpu
from jax.sharding import Mesh
from jax.sharding import PartitionSpec as P

LAT = ("x_hi", "z_hi", "z_lo", "core")
LON = ("y_hi", "y_lo", "x_lo")
NEAR = ("x_hi", "z_lo", "y_lo", "x_lo")
FAR = ("z_hi", "y_hi")
CORE = ("core",)
LANES = 128
CHUNK = 256
BF16 = jnp.bfloat16
F32 = jnp.float32


def exchange(part, axes):
    return lax.all_to_all(part, axes, 0, 0, tiled=True)


def reduce_stage(part, axes):
    got = exchange(part, axes)
    count = lax.axis_size(axes)
    return jnp.sum(got.reshape(count, -1, got.shape[-1]).astype(F32), axis=0)


def gather_stage(part, axes):
    count = lax.axis_size(axes)
    copies = jnp.broadcast_to(part[None], (count,) + part.shape)
    return exchange(copies.reshape(-1, part.shape[-1]), axes)


def all_sum(part, scale):
    features = part.shape[-1]
    tiles = features // LANES
    part = reduce_stage(part, CORE).astype(BF16)
    part = reduce_stage(part, NEAR).astype(BF16)
    rows = part.shape[0]
    part = part.reshape(rows, tiles, LANES).transpose(1, 0, 2).reshape(-1, LANES)
    part = (reduce_stage(part, FAR) * scale).astype(BF16)
    part = gather_stage(part, FAR)
    part = part.reshape(tiles, rows, LANES).transpose(1, 0, 2).reshape(rows, features)
    part = gather_stage(part, NEAR)
    return gather_stage(part, CORE)


def both_ways(block, axis):
    count = lax.axis_size(axis)
    forward = [(i, i + 1) for i in range(count - 1)]
    backward = [(target, source) for source, target in forward]
    return lax.ppermute(block, axis, forward), lax.ppermute(block, axis, backward)


def silu_parts(values):
    sigmoid_v = jax.nn.sigmoid(values)
    return values * sigmoid_v, sigmoid_v * (1.0 + values * (1.0 - sigmoid_v))


def mm(left, right):
    return lax.dot_general(left, right, (((1,), (0,)), ((), ())), preferred_element_type=F32)


def mm_rows(left, right):
    return lax.dot_general(left, right, (((0,), (0,)), ((), ())), preferred_element_type=F32)


def mm_cols(left, right):
    return lax.dot_general(left, right, (((1,), (1,)), ((), ())), preferred_element_type=F32)


def column(row):
    return jnp.transpose(jnp.broadcast_to(row, (8, row.shape[-1])))[:, :1]


def one_hot_cols(ids_column, width):
    lane_ids = lax.broadcasted_iota(jnp.int32, (ids_column.shape[0], width), 1)
    return (ids_column == lane_ids).astype(F32).astype(BF16)


def one_hot_rows(ids_row, height):
    row_ids = lax.broadcasted_iota(jnp.int32, (height, ids_row.shape[-1]), 0)
    return (ids_row == row_ids).astype(F32).astype(BF16)


def block_kernel(
    low_ref,
    mid_ref,
    high_ref,
    nodes_ref,
    top_ref,
    cot_ref,
    w_src_ref,
    w_dst_ref,
    w_msg_ref,
    w_top_ref,
    src_ref,
    dst_ref,
    band_ref,
    updated_ref,
    grads_ref,
    window_ref,
    ext,
    picked,
    hidden,
    pre_grad,
    act_grad,
    act_slope,
    msg_slope,
    dst_cols,
    w_src,
    w_dst,
    w_msg,
    w_top,
    nodes_own,
    top_own,
    cot_own,
    arrived,
):
    held = (w_src, w_dst, w_msg, w_top, nodes_own, top_own, cot_own)
    sources = (w_src_ref, w_dst_ref, w_msg_ref, w_top_ref, nodes_ref, top_ref, cot_ref)
    copies = [
        pltpu.make_async_copy(source, target, arrived.at[place])
        for place, (source, target) in enumerate(zip(sources, held))
    ]
    for place in (4, 0, 1, 2, 3, 5, 6):
        copies[place].start()
    slots = src_ref.shape[-1]
    block, features = nodes_own.shape
    third = low_ref.shape[0]
    ext[0:third, :] = low_ref[...]
    ext[third : 2 * third, :] = mid_ref[...]
    ext[2 * third :, :] = high_ref[...]
    src_col = column(src_ref[...])
    dst_col = column(dst_ref[...])
    dst_rows = one_hot_rows(dst_ref[...], block)
    inflow = jnp.zeros((block, features), F32)
    for start in range(0, slots, CHUNK):
        span = slice(start, start + CHUNK)
        gathered = mm(one_hot_cols(src_col[span], ext.shape[0]), ext[...]).astype(BF16)
        picked[span, :] = gathered
        if start == 0:
            for place in (4, 0, 1, 2):
                copies[place].wait()
            nodes = nodes_own[...]
        at_dst = one_hot_cols(dst_col[span], block)
        dst_cols[span, :] = at_dst
        local = mm(at_dst, nodes).astype(BF16)
        pre_act = mm(gathered, w_src[...]) + mm(local, w_dst[...])
        value, slope = silu_parts(pre_act)
        act_slope[span, :] = slope
        hid = value.astype(BF16)
        hidden[span, :] = hid
        value, slope = silu_parts(mm(hid, w_msg[...]))
        msg_slope[span, :] = slope
        inflow = inflow + mm(dst_rows[:, span], value.astype(BF16))
    for place in (3, 5, 6):
        copies[place].wait()
    top_count = top_own.shape[0]
    top_nodes = top_own[...]
    top_table = mm(top_nodes, w_top[...]).astype(BF16)
    band_col = column(band_ref[...])
    node_pre = inflow + mm(one_hot_cols(band_col, top_count), top_table)
    value, slope = silu_parts(node_pre)
    updated_ref[...] = (nodes.astype(F32) + value).astype(BF16)
    node_grad = (cot_own[...].astype(F32) * slope).astype(BF16)
    window = mm(one_hot_rows(band_ref[...], top_count), node_grad)
    window_ref[...] = window
    grads_ref[3] = mm_rows(top_nodes, window.astype(BF16)).astype(BF16)
    dst_grad = jnp.zeros((block, features), F32)
    for start in range(0, slots, CHUNK):
        span = slice(start, start + CHUNK)
        msg_grad = mm(dst_cols[span, :], node_grad)
        grad = (msg_grad * msg_slope[span, :]).astype(BF16)
        pre_grad[span, :] = grad
        grad = (mm_cols(grad, w_msg[...]) * act_slope[span, :]).astype(BF16)
        act_grad[span, :] = grad
        dst_grad = dst_grad + mm(dst_rows[:, span], grad)
    grads_ref[0] = mm_rows(picked[...], act_grad[...]).astype(BF16)
    grads_ref[1] = mm_rows(nodes, dst_grad.astype(BF16)).astype(BF16)
    grads_ref[2] = mm_rows(hidden[...], pre_grad[...]).astype(BF16)


def block_round(*args):
    nodes, top_nodes = args[3], args[4]
    slots = args[10].shape[-1]
    block, features = nodes.shape
    ext_rows = 3 * args[0].shape[0]
    hbm = pltpu.MemorySpace.HBM
    stay = [pltpu.with_memory_space_constraint(array, hbm) for array in args[3:10]]
    return pl.pallas_call(
        block_kernel,
        out_shape=(
            jax.ShapeDtypeStruct((block, features), BF16),
            jax.ShapeDtypeStruct((4, features, features), BF16),
            jax.ShapeDtypeStruct((top_nodes.shape[0], features), F32),
        ),
        scratch_shapes=[
            pltpu.VMEM((ext_rows, features), BF16),
            pltpu.VMEM((slots, features), BF16),
            pltpu.VMEM((slots, features), BF16),
            pltpu.VMEM((slots, features), BF16),
            pltpu.VMEM((slots, features), BF16),
            pltpu.VMEM((slots, features), F32),
            pltpu.VMEM((slots, features), F32),
            pltpu.VMEM((slots, block), BF16),
            pltpu.VMEM((features, features), BF16),
            pltpu.VMEM((features, features), BF16),
            pltpu.VMEM((features, features), BF16),
            pltpu.VMEM((features, features), BF16),
            pltpu.VMEM((block, features), BF16),
            pltpu.VMEM(top_nodes.shape, BF16),
            pltpu.VMEM((block, features), BF16),
            pltpu.SemaphoreType.DMA((7,)),
        ],
        in_specs=[pl.BlockSpec(memory_space=pltpu.MemorySpace.VMEM)] * 3
        + [pl.BlockSpec(memory_space=pltpu.MemorySpace.HBM)] * 7
        + [pl.BlockSpec(memory_space=pltpu.MemorySpace.VMEM)] * 3,
        compiler_params=pltpu.CompilerParams(vmem_limit_bytes=48 << 20),
        name="block_round",
    )(*args[:3], *stay, *args[10:])


def shards(
    nodes,
    top_nodes,
    cotangent,
    w_src,
    w_dst,
    w_msg,
    w_top,
    src_code,
    src_node,
    dst_node,
    edge_count,
    parent,
):
    block_size, features = nodes.shape[2:]
    slots = src_code.shape[-1]
    top_local = top_nodes.shape[0]
    owner_rows = top_local // lax.axis_size(LON)
    lon_index = lax.axis_index(LON)
    band_start = lax.axis_index(LAT) * top_local
    own = nodes.reshape(block_size, features)
    west, east = both_ways(own, LON)
    mid = jnp.concatenate([west, own, east], axis=0)
    low, high = both_ways(mid, LAT)
    src_idx = (src_code * block_size + src_node).reshape(1, slots)
    live_slot = lax.broadcasted_iota(jnp.int32, (1, slots), 1) < edge_count
    dst_idx = jnp.where(live_slot, dst_node.reshape(1, slots), block_size)
    band_ids = parent.reshape(1, block_size) - band_start
    updated, grads, window = block_round(
        low,
        mid,
        high,
        own,
        top_nodes,
        cotangent.reshape(block_size, features),
        w_src,
        w_dst,
        w_msg,
        w_top,
        src_idx,
        dst_idx,
        band_ids,
    )
    nodes_total = block_size * lax.axis_size(LAT) * lax.axis_size(LON)
    grad_scale = 8.0 / math.sqrt(nodes_total)
    weight_grads = all_sum(grads.reshape(-1, features), grad_scale)
    padded = jnp.pad(window, ((owner_rows, owner_rows), (0, 0)))
    triple = lax.dynamic_slice_in_dim(padded, lon_index * owner_rows, 3 * owner_rows, 0)
    count = lax.axis_size(LON)
    forward = [(i, i + 1) for i in range(count - 1)]
    backward = [(target, source) for source, target in forward]
    from_left = lax.ppermute(triple[2 * owner_rows :], LON, forward)
    from_right = lax.ppermute(triple[:owner_rows], LON, backward)
    table_grad = (triple[owner_rows : 2 * owner_rows] + from_left + from_right).astype(BF16)
    d_top = lax.dot_general(
        table_grad, w_top, (((1,), (1,)), ((), ())), preferred_element_type=F32
    ).astype(BF16)
    return (
        updated.reshape(nodes.shape),
        weight_grads.reshape(4, features, features),
        d_top,
    )


def solution(mesh):
    lat_count, lon_count = mesh.shape["lat"], mesh.shape["lon"]
    fine = Mesh(
        mesh.devices.reshape(2, lat_count // 8, 2, 2, lon_count // 4, 2, 2),
        LAT + LON,
    )
    placed = (
        P(LAT, LON, None, None),
        P(LAT, None),
        P(LAT, LON, None, None),
        P(),
        P(),
        P(),
        P(),
        P(LAT, LON, None),
        P(LAT, LON, None),
        P(LAT, LON, None),
        P(LAT, LON),
        P(LAT, LON, None),
    )
    return jax.shard_map(
        shards,
        mesh=fine,
        in_specs=placed,
        out_specs=(P(LAT, LON, None, None), P(), P(LAT + LON, None)),
        check_vma=False,
    )
```

```python
import math

import jax
import jax.numpy as jnp
from jax import lax
from jax.experimental import pallas as pl
from jax.experimental.pallas import tpu as pltpu
from jax.sharding import Mesh
from jax.sharding import PartitionSpec as P

LAT = ("x_hi", "z_hi", "z_lo", "core")
LON = ("y_hi", "y_lo", "x_lo")
RING_X = ("x_hi", "x_lo")
RING_Y = ("y_hi", "y_lo")
RING_Z = ("z_hi", "z_lo")
CHUNK = 256
BF16 = jnp.bfloat16
F32 = jnp.float32


def exchange(part, axes):
    return lax.all_to_all(part, axes, 0, 0, tiled=True)


def reduce_stage(part, axes):
    got = exchange(part, axes)
    count = lax.axis_size(axes)
    return jnp.sum(got.reshape(count, -1, got.shape[-1]).astype(F32), axis=0)


def gather_stage(part, axes):
    count = lax.axis_size(axes)
    copies = jnp.broadcast_to(part[None], (count,) + part.shape)
    return exchange(copies.reshape(-1, part.shape[-1]), axes)


def swap_cores(part):
    return lax.ppermute(part, "core", [(0, 1), (1, 0)])


def reduce_all(keep, send, scale):
    part = (keep.astype(F32) + swap_cores(send).astype(F32)).astype(BF16)
    part = reduce_stage(part, RING_X).astype(BF16)
    part = reduce_stage(part, RING_Y).astype(BF16)
    every = gather_stage(part, RING_Z).reshape((-1,) + part.shape)
    part = (jnp.sum(every.astype(F32), axis=0) * scale).astype(BF16)
    return gather_stage(part, RING_Y)


def place_kernel(mine_ref, other_ref, core_ref, out_ref, placed):
    core = core_ref[0]
    first = pltpu.make_async_copy(mine_ref, out_ref.at[core], placed.at[0])
    second = pltpu.make_async_copy(other_ref, out_ref.at[1 - core], placed.at[1])
    first.start()
    second.start()
    first.wait()
    second.wait()


def both_halves(mine):
    other = swap_cores(mine)
    vmem = pl.BlockSpec(memory_space=pltpu.MemorySpace.VMEM)
    return pl.pallas_call(
        place_kernel,
        out_shape=jax.ShapeDtypeStruct((2,) + mine.shape, mine.dtype),
        in_specs=[vmem, vmem, pl.BlockSpec(memory_space=pltpu.MemorySpace.SMEM)],
        out_specs=pl.BlockSpec(memory_space=pltpu.MemorySpace.HBM),
        scratch_shapes=[pltpu.SemaphoreType.DMA((2,))],
        name="both_halves",
    )(mine, other, lax.axis_index("core").reshape(1))


def both_ways(block, axis):
    count = lax.axis_size(axis)
    forward = [(i, i + 1) for i in range(count - 1)]
    backward = [(target, source) for source, target in forward]
    return lax.ppermute(block, axis, forward), lax.ppermute(block, axis, backward)


def silu_parts(values):
    sigmoid_v = jax.nn.sigmoid(values)
    return values * sigmoid_v, sigmoid_v * (1.0 + values * (1.0 - sigmoid_v))


def mm(left, right):
    return lax.dot_general(left, right, (((1,), (0,)), ((), ())), preferred_element_type=F32)


def mm_rows(left, right):
    return lax.dot_general(left, right, (((0,), (0,)), ((), ())), preferred_element_type=F32)


def mm_cols(left, right):
    return lax.dot_general(left, right, (((1,), (1,)), ((), ())), preferred_element_type=F32)


def column(row):
    return jnp.transpose(jnp.broadcast_to(row, (8, row.shape[-1])))[:, :1]


def one_hot_cols(ids_column, width):
    lane_ids = lax.broadcasted_iota(jnp.int32, (ids_column.shape[0], width), 1)
    return (ids_column == lane_ids).astype(F32).astype(BF16)


def one_hot_rows(ids_row, height):
    row_ids = lax.broadcasted_iota(jnp.int32, (height, ids_row.shape[-1]), 0)
    return (ids_row == row_ids).astype(F32).astype(BF16)


def block_kernel(
    low_ref,
    mid_ref,
    high_ref,
    nodes_ref,
    top_ref,
    cot_ref,
    w_src_ref,
    w_dst_ref,
    w_msg_ref,
    w_top_ref,
    src_ref,
    dst_ref,
    band_ref,
    core_ref,
    updated_ref,
    keep_ref,
    send_ref,
    window_ref,
    ext,
    picked,
    hidden,
    pre_grad,
    act_grad,
    act_slope,
    msg_slope,
    dst_cols,
    w_src,
    w_dst,
    w_msg,
    w_top,
    nodes_own,
    top_own,
    cot_own,
    arrived,
):
    core = core_ref[0]

    def emit(place, grad):
        @pl.when(core == place // 2)
        def _():
            keep_ref[place % 2] = grad

        @pl.when(core != place // 2)
        def _():
            send_ref[place % 2] = grad

    held = (w_src, w_dst, w_msg, w_top, nodes_own, top_own, cot_own)
    sources = (w_src_ref, w_dst_ref, w_msg_ref, w_top_ref, nodes_ref, top_ref, cot_ref)
    copies = [
        pltpu.make_async_copy(source, target, arrived.at[place])
        for place, (source, target) in enumerate(zip(sources, held))
    ]
    for place in (4, 0, 1, 2, 3, 5, 6):
        copies[place].start()
    slots = src_ref.shape[-1]
    block, features = nodes_own.shape
    third = low_ref.shape[0]
    ext[0:third, :] = low_ref[...]
    ext[third : 2 * third, :] = mid_ref[...]
    ext[2 * third :, :] = high_ref[...]
    src_col = column(src_ref[...])
    dst_col = column(dst_ref[...])
    dst_rows = one_hot_rows(dst_ref[...], block)
    inflow = jnp.zeros((block, features), F32)
    for start in range(0, slots, CHUNK):
        span = slice(start, start + CHUNK)
        gathered = mm(one_hot_cols(src_col[span], ext.shape[0]), ext[...]).astype(BF16)
        picked[span, :] = gathered
        if start == 0:
            for place in (4, 0, 1, 2):
                copies[place].wait()
            nodes = nodes_own[...]
        at_dst = one_hot_cols(dst_col[span], block)
        dst_cols[span, :] = at_dst
        local = mm(at_dst, nodes).astype(BF16)
        pre_act = mm(gathered, w_src[...]) + mm(local, w_dst[...])
        value, slope = silu_parts(pre_act)
        act_slope[span, :] = slope
        hid = value.astype(BF16)
        hidden[span, :] = hid
        value, slope = silu_parts(mm(hid, w_msg[...]))
        msg_slope[span, :] = slope
        inflow = inflow + mm(dst_rows[:, span], value.astype(BF16))
    for place in (3, 5, 6):
        copies[place].wait()
    top_count = top_own.shape[0]
    top_nodes = top_own[...]
    top_table = mm(top_nodes, w_top[...]).astype(BF16)
    band_col = column(band_ref[...])
    node_pre = inflow + mm(one_hot_cols(band_col, top_count), top_table)
    value, slope = silu_parts(node_pre)
    updated_ref[...] = (nodes.astype(F32) + value).astype(BF16)
    node_grad = (cot_own[...].astype(F32) * slope).astype(BF16)
    window = mm(one_hot_rows(band_ref[...], top_count), node_grad)
    window_ref[...] = window
    emit(3, mm_rows(top_nodes, window.astype(BF16)).astype(BF16))
    dst_grad = jnp.zeros((block, features), F32)
    for start in range(0, slots, CHUNK):
        span = slice(start, start + CHUNK)
        msg_grad = mm(dst_cols[span, :], node_grad)
        grad = (msg_grad * msg_slope[span, :]).astype(BF16)
        pre_grad[span, :] = grad
        grad = (mm_cols(grad, w_msg[...]) * act_slope[span, :]).astype(BF16)
        act_grad[span, :] = grad
        dst_grad = dst_grad + mm(dst_rows[:, span], grad)
    emit(0, mm_rows(picked[...], act_grad[...]).astype(BF16))
    emit(1, mm_rows(nodes, dst_grad.astype(BF16)).astype(BF16))
    emit(2, mm_rows(hidden[...], pre_grad[...]).astype(BF16))


def block_round(*args):
    nodes, top_nodes = args[3], args[4]
    slots = args[10].shape[-1]
    block, features = nodes.shape
    ext_rows = 3 * args[0].shape[0]
    hbm = pltpu.MemorySpace.HBM
    stay = [pltpu.with_memory_space_constraint(array, hbm) for array in args[3:10]]
    return pl.pallas_call(
        block_kernel,
        out_shape=(
            jax.ShapeDtypeStruct((block, features), BF16),
            jax.ShapeDtypeStruct((2, features, features), BF16),
            jax.ShapeDtypeStruct((2, features, features), BF16),
            jax.ShapeDtypeStruct((top_nodes.shape[0], features), F32),
        ),
        scratch_shapes=[
            pltpu.VMEM((ext_rows, features), BF16),
            pltpu.VMEM((slots, features), BF16),
            pltpu.VMEM((slots, features), BF16),
            pltpu.VMEM((slots, features), BF16),
            pltpu.VMEM((slots, features), BF16),
            pltpu.VMEM((slots, features), F32),
            pltpu.VMEM((slots, features), F32),
            pltpu.VMEM((slots, block), BF16),
            pltpu.VMEM((features, features), BF16),
            pltpu.VMEM((features, features), BF16),
            pltpu.VMEM((features, features), BF16),
            pltpu.VMEM((features, features), BF16),
            pltpu.VMEM((block, features), BF16),
            pltpu.VMEM(top_nodes.shape, BF16),
            pltpu.VMEM((block, features), BF16),
            pltpu.SemaphoreType.DMA((7,)),
        ],
        in_specs=[pl.BlockSpec(memory_space=pltpu.MemorySpace.VMEM)] * 3
        + [pl.BlockSpec(memory_space=pltpu.MemorySpace.HBM)] * 7
        + [pl.BlockSpec(memory_space=pltpu.MemorySpace.VMEM)] * 3
        + [pl.BlockSpec(memory_space=pltpu.MemorySpace.SMEM)],
        compiler_params=pltpu.CompilerParams(vmem_limit_bytes=48 << 20),
        name="block_round",
    )(*args[:3], *stay, *args[10:])


def shards(
    nodes,
    top_nodes,
    cotangent,
    w_src,
    w_dst,
    w_msg,
    w_top,
    src_code,
    src_node,
    dst_node,
    edge_count,
    parent,
):
    block_size, features = nodes.shape[2:]
    slots = src_code.shape[-1]
    top_local = top_nodes.shape[0]
    owner_rows = top_local // lax.axis_size(LON)
    lon_index = lax.axis_index(LON)
    band_start = lax.axis_index(LAT) * top_local
    own = nodes.reshape(block_size, features)
    west, east = both_ways(own, LON)
    mid = jnp.concatenate([west, own, east], axis=0)
    low, high = both_ways(mid, LAT)
    src_idx = (src_code * block_size + src_node).reshape(1, slots)
    live_slot = lax.broadcasted_iota(jnp.int32, (1, slots), 1) < edge_count
    dst_idx = jnp.where(live_slot, dst_node.reshape(1, slots), block_size)
    band_ids = parent.reshape(1, block_size) - band_start
    updated, keep, send, window = block_round(
        low,
        mid,
        high,
        own,
        top_nodes,
        cotangent.reshape(block_size, features),
        w_src,
        w_dst,
        w_msg,
        w_top,
        src_idx,
        dst_idx,
        band_ids,
        lax.axis_index("core").reshape(1),
    )
    nodes_total = block_size * lax.axis_size(LAT) * lax.axis_size(LON)
    grad_scale = 8.0 / math.sqrt(nodes_total)
    quarter = reduce_all(keep.reshape(-1, features), send.reshape(-1, features), grad_scale)
    window, quarter = lax.optimization_barrier((window, quarter))
    mine = gather_stage(quarter, RING_X)
    padded = jnp.pad(window, ((owner_rows, owner_rows), (0, 0)))
    triple = lax.dynamic_slice_in_dim(padded, lon_index * owner_rows, 3 * owner_rows, 0)
    count = lax.axis_size(LON)
    forward = [(i, i + 1) for i in range(count - 1)]
    backward = [(target, source) for source, target in forward]
    from_left = lax.ppermute(triple[2 * owner_rows :], LON, forward)
    from_right = lax.ppermute(triple[:owner_rows], LON, backward)
    mine, from_left, from_right = lax.optimization_barrier((mine, from_left, from_right))
    weight_grads = both_halves(mine)
    table_grad = (triple[owner_rows : 2 * owner_rows] + from_left + from_right).astype(BF16)
    d_top = lax.dot_general(
        table_grad, w_top, (((1,), (1,)), ((), ())), preferred_element_type=F32
    ).astype(BF16)
    return (
        updated.reshape(nodes.shape),
        weight_grads.reshape(4, features, features),
        d_top,
    )


def solution(mesh):
    lat_count, lon_count = mesh.shape["lat"], mesh.shape["lon"]
    fine = Mesh(
        mesh.devices.reshape(2, lat_count // 8, 2, 2, lon_count // 4, 2, 2),
        LAT + LON,
    )
    placed = (
        P(LAT, LON, None, None),
        P(LAT, None),
        P(LAT, LON, None, None),
        P(),
        P(),
        P(),
        P(),
        P(LAT, LON, None),
        P(LAT, LON, None),
        P(LAT, LON, None),
        P(LAT, LON),
        P(LAT, LON, None),
    )
    return jax.shard_map(
        shards,
        mesh=fine,
        in_specs=placed,
        out_specs=(P(LAT, LON, None, None), P(), P(LAT + LON, None)),
        check_vma=False,
    )
```

```python
import math

import jax
import jax.numpy as jnp
from jax import lax
from jax.experimental import pallas as pl
from jax.experimental.pallas import tpu as pltpu
from jax.sharding import Mesh
from jax.sharding import PartitionSpec as P

LAT = ("x_hi", "z_hi", "z_lo", "core")
LON = ("y_hi", "y_lo", "x_lo")
RING_X = ("x_hi", "x_lo")
RING_Y = ("y_hi", "y_lo")
RING_Z = ("z_hi", "z_lo")
CORE = ("core",)
CHUNK = 256
BF16 = jnp.bfloat16
F32 = jnp.float32


def exchange(part, axes):
    return lax.all_to_all(part, axes, 0, 0, tiled=True)


def reduce_stage(part, axes):
    got = exchange(part, axes)
    count = lax.axis_size(axes)
    return jnp.sum(got.reshape(count, -1, got.shape[-1]).astype(F32), axis=0)


def gather_stage(part, axes):
    count = lax.axis_size(axes)
    copies = jnp.broadcast_to(part[None], (count,) + part.shape)
    return exchange(copies.reshape(-1, part.shape[-1]), axes)


def ring_z_sum(part):
    every = gather_stage(part, RING_Z).reshape((-1,) + part.shape)
    return jnp.sum(every.astype(F32), axis=0)


def inner_swap(block, axis):
    count = lax.axis_size(axis)
    return lax.ppermute(block, axis, [(i, i ^ 1) for i in range(count)])


def outer_swap(block, axis):
    count = lax.axis_size(axis)
    partner = {i: i + 1 if i % 2 else i - 1 for i in range(count)}
    return lax.ppermute(block, axis, [(i, j) for i, j in partner.items() if 0 <= j < count])


def silu_parts(values):
    sigmoid_v = jax.nn.sigmoid(values)
    return values * sigmoid_v, sigmoid_v * (1.0 + values * (1.0 - sigmoid_v))


def mm(left, right):
    return lax.dot_general(left, right, (((1,), (0,)), ((), ())), preferred_element_type=F32)


def mm_rows(left, right):
    return lax.dot_general(left, right, (((0,), (0,)), ((), ())), preferred_element_type=F32)


def mm_cols(left, right):
    return lax.dot_general(left, right, (((1,), (1,)), ((), ())), preferred_element_type=F32)


def column(row):
    return jnp.transpose(jnp.broadcast_to(row, (8, row.shape[-1])))[:, :1]


def one_hot_cols(ids_column, width):
    lane_ids = lax.broadcasted_iota(jnp.int32, (ids_column.shape[0], width), 1)
    return (ids_column == lane_ids).astype(F32).astype(BF16)


def one_hot_rows(ids_row, height):
    row_ids = lax.broadcasted_iota(jnp.int32, (height, ids_row.shape[-1]), 0)
    return (ids_row == row_ids).astype(F32).astype(BF16)


def block_kernel(
    low_ref,
    mid_ref,
    high_ref,
    nodes_ref,
    top_ref,
    cot_ref,
    w_src_ref,
    w_dst_ref,
    w_msg_ref,
    w_top_ref,
    src_ref,
    dst_ref,
    band_ref,
    updated_ref,
    grads_ref,
    window_ref,
    ext,
    picked,
    hidden,
    pre_grad,
    act_grad,
    act_slope,
    msg_slope,
    dst_cols,
    w_src,
    w_dst,
    w_msg,
    w_top,
    nodes_own,
    top_own,
    cot_own,
    arrived,
):
    held = (w_src, w_dst, w_msg, w_top, nodes_own, top_own, cot_own)
    sources = (w_src_ref, w_dst_ref, w_msg_ref, w_top_ref, nodes_ref, top_ref, cot_ref)
    copies = [
        pltpu.make_async_copy(source, target, arrived.at[place])
        for place, (source, target) in enumerate(zip(sources, held))
    ]
    for place in (4, 0, 1, 2, 3, 5, 6):
        copies[place].start()
    slots = src_ref.shape[-1]
    block, features = nodes_own.shape
    third = low_ref.shape[0]
    ext[0:third, :] = low_ref[...]
    ext[third : 2 * third, :] = mid_ref[...]
    ext[2 * third :, :] = high_ref[...]
    src_col = column(src_ref[...])
    dst_col = column(dst_ref[...])
    dst_rows = one_hot_rows(dst_ref[...], block)
    inflow = jnp.zeros((block, features), F32)
    for start in range(0, slots, CHUNK):
        span = slice(start, start + CHUNK)
        gathered = mm(one_hot_cols(src_col[span], ext.shape[0]), ext[...]).astype(BF16)
        picked[span, :] = gathered
        if start == 0:
            for place in (4, 0, 1, 2):
                copies[place].wait()
            nodes = nodes_own[...]
        at_dst = one_hot_cols(dst_col[span], block)
        dst_cols[span, :] = at_dst
        local = mm(at_dst, nodes).astype(BF16)
        pre_act = mm(gathered, w_src[...]) + mm(local, w_dst[...])
        value, slope = silu_parts(pre_act)
        act_slope[span, :] = slope
        hid = value.astype(BF16)
        hidden[span, :] = hid
        value, slope = silu_parts(mm(hid, w_msg[...]))
        msg_slope[span, :] = slope
        inflow = inflow + mm(dst_rows[:, span], value.astype(BF16))
    for place in (3, 5, 6):
        copies[place].wait()
    top_count = top_own.shape[0]
    top_nodes = top_own[...]
    top_table = mm(top_nodes, w_top[...]).astype(BF16)
    band_col = column(band_ref[...])
    node_pre = inflow + mm(one_hot_cols(band_col, top_count), top_table)
    value, slope = silu_parts(node_pre)
    updated_ref[...] = (nodes.astype(F32) + value).astype(BF16)
    node_grad = (cot_own[...].astype(F32) * slope).astype(BF16)
    window = mm(one_hot_rows(band_ref[...], top_count), node_grad)
    window_ref[...] = window
    grads_ref[3] = mm_rows(top_nodes, window.astype(BF16)).astype(BF16)
    dst_grad = jnp.zeros((block, features), F32)
    for start in range(0, slots, CHUNK):
        span = slice(start, start + CHUNK)
        msg_grad = mm(dst_cols[span, :], node_grad)
        grad = (msg_grad * msg_slope[span, :]).astype(BF16)
        pre_grad[span, :] = grad
        grad = (mm_cols(grad, w_msg[...]) * act_slope[span, :]).astype(BF16)
        act_grad[span, :] = grad
        dst_grad = dst_grad + mm(dst_rows[:, span], grad)
    grads_ref[0] = mm_rows(picked[...], act_grad[...]).astype(BF16)
    grads_ref[1] = mm_rows(nodes, dst_grad.astype(BF16)).astype(BF16)
    grads_ref[2] = mm_rows(hidden[...], pre_grad[...]).astype(BF16)


def block_round(*args):
    nodes, top_nodes = args[3], args[4]
    slots = args[10].shape[-1]
    block, features = nodes.shape
    ext_rows = 3 * args[0].shape[0]
    hbm = pltpu.MemorySpace.HBM
    stay = [pltpu.with_memory_space_constraint(array, hbm) for array in args[3:10]]
    return pl.pallas_call(
        block_kernel,
        out_shape=(
            jax.ShapeDtypeStruct((block, features), BF16),
            jax.ShapeDtypeStruct((4, features, features), BF16),
            jax.ShapeDtypeStruct((top_nodes.shape[0], features), F32),
        ),
        scratch_shapes=[
            pltpu.VMEM((ext_rows, features), BF16),
            pltpu.VMEM((slots, features), BF16),
            pltpu.VMEM((slots, features), BF16),
            pltpu.VMEM((slots, features), BF16),
            pltpu.VMEM((slots, features), BF16),
            pltpu.VMEM((slots, features), F32),
            pltpu.VMEM((slots, features), F32),
            pltpu.VMEM((slots, block), BF16),
            pltpu.VMEM((features, features), BF16),
            pltpu.VMEM((features, features), BF16),
            pltpu.VMEM((features, features), BF16),
            pltpu.VMEM((features, features), BF16),
            pltpu.VMEM((block, features), BF16),
            pltpu.VMEM(top_nodes.shape, BF16),
            pltpu.VMEM((block, features), BF16),
            pltpu.SemaphoreType.DMA((7,)),
        ],
        in_specs=[pl.BlockSpec(memory_space=pltpu.MemorySpace.VMEM)] * 3
        + [pl.BlockSpec(memory_space=pltpu.MemorySpace.HBM)] * 7
        + [pl.BlockSpec(memory_space=pltpu.MemorySpace.VMEM)] * 3,
        compiler_params=pltpu.CompilerParams(vmem_limit_bytes=48 << 20),
        name="block_round",
    )(*args[:3], *stay, *args[10:])


def shards(
    nodes,
    top_nodes,
    cotangent,
    w_src,
    w_dst,
    w_msg,
    w_top,
    src_code,
    src_node,
    dst_node,
    edge_count,
    parent,
):
    block_size, features = nodes.shape[2:]
    slots = src_code.shape[-1]
    top_local = top_nodes.shape[0]
    owner_rows = top_local // lax.axis_size(LON)
    lon_index = lax.axis_index(LON)
    band_start = lax.axis_index(LAT) * top_local
    own = nodes.reshape(block_size, features)
    lat_odd, lon_odd = lax.axis_index("core"), lax.axis_index("x_lo")
    outer = outer_swap(own, LON)
    inner = inner_swap(own, LON)
    mid = jnp.concatenate([outer, own, inner], axis=0)
    low = outer_swap(mid, LAT)
    high = inner_swap(mid, LAT)
    src_row, src_col = src_code // 3, src_code % 3
    src_row = jnp.where(lat_odd == 1, 2 - src_row, src_row)
    src_col = jnp.where(lon_odd == 1, 2 - src_col, src_col)
    src_idx = ((src_row * 3 + src_col) * block_size + src_node).reshape(1, slots)
    live_slot = lax.broadcasted_iota(jnp.int32, (1, slots), 1) < edge_count
    dst_idx = jnp.where(live_slot, dst_node.reshape(1, slots), block_size)
    band_ids = parent.reshape(1, block_size) - band_start
    updated, grads, window = block_round(
        low,
        mid,
        high,
        own,
        top_nodes,
        cotangent.reshape(block_size, features),
        w_src,
        w_dst,
        w_msg,
        w_top,
        src_idx,
        dst_idx,
        band_ids,
    )
    nodes_total = block_size * lax.axis_size(LAT) * lax.axis_size(LON)
    grad_scale = 8.0 / math.sqrt(nodes_total)
    part = reduce_stage(grads.reshape(-1, features), CORE).astype(BF16)
    part = reduce_stage(part, RING_X).astype(BF16)
    part = reduce_stage(part, RING_Y).astype(BF16)
    window, part = lax.optimization_barrier((window, part))
    padded = jnp.pad(window, ((owner_rows, owner_rows), (0, 0)))
    triple = lax.dynamic_slice_in_dim(padded, lon_index * owner_rows, 3 * owner_rows, 0)
    left, centre, right = jnp.split(triple, 3)
    from_inner = inner_swap(jnp.where(lon_odd == 1, left, right), LON)
    total = ring_z_sum(part)
    total, from_inner, left, right = lax.optimization_barrier((total, from_inner, left, right))
    from_outer = outer_swap(jnp.where(lon_odd == 1, right, left), LON)
    part = gather_stage((total * grad_scale).astype(BF16), RING_Y)
    part, from_outer = lax.optimization_barrier((part, from_outer))
    part = gather_stage(part, RING_X)
    weight_grads = gather_stage(part, CORE)
    table_grad = (centre + from_inner + from_outer).astype(BF16)
    d_top = lax.dot_general(
        table_grad, w_top, (((1,), (1,)), ((), ())), preferred_element_type=F32
    ).astype(BF16)
    return (
        updated.reshape(nodes.shape),
        weight_grads.reshape(4, features, features),
        d_top,
    )


def solution(mesh):
    lat_count, lon_count = mesh.shape["lat"], mesh.shape["lon"]
    fine = Mesh(
        mesh.devices.reshape(2, lat_count // 8, 2, 2, lon_count // 4, 2, 2),
        LAT + LON,
    )
    placed = (
        P(LAT, LON, None, None),
        P(LAT, None),
        P(LAT, LON, None, None),
        P(),
        P(),
        P(),
        P(),
        P(LAT, LON, None),
        P(LAT, LON, None),
        P(LAT, LON, None),
        P(LAT, LON),
        P(LAT, LON, None),
    )
    return jax.shard_map(
        shards,
        mesh=fine,
        in_specs=placed,
        out_specs=(P(LAT, LON, None, None), P(), P(LAT + LON, None)),
        check_vma=False,
    )
```

```python
import math

import jax
import jax.numpy as jnp
from jax import lax
from jax.experimental import pallas as pl
from jax.experimental.pallas import tpu as pltpu
from jax.sharding import Mesh
from jax.sharding import PartitionSpec as P

LAT = ("x_hi", "z_hi", "z_lo", "core")
LON = ("y_hi", "y_lo", "x_lo")
NEAR = ("x_hi", "z_lo", "y_lo", "x_lo")
FAR = ("z_hi", "y_hi")
CORE = ("core",)
LANES = 128
CHUNK = 256
BF16 = jnp.bfloat16
F32 = jnp.float32


def exchange(part, axes):
    return lax.all_to_all(part, axes, 0, 0, tiled=True)


def reduce_stage(part, axes):
    got = exchange(part, axes)
    count = lax.axis_size(axes)
    return jnp.sum(got.reshape(count, -1, got.shape[-1]).astype(F32), axis=0)


def gather_stage(part, axes):
    count = lax.axis_size(axes)
    copies = jnp.broadcast_to(part[None], (count,) + part.shape)
    return exchange(copies.reshape(-1, part.shape[-1]), axes)


def far_sum(part, scale):
    rows, features = part.shape
    tiles = features // LANES
    part = part.reshape(rows, tiles, LANES).transpose(1, 0, 2).reshape(-1, LANES)
    part = gather_stage((reduce_stage(part, FAR) * scale).astype(BF16), FAR)
    return part.reshape(tiles, rows, LANES).transpose(1, 0, 2).reshape(rows, features)


def inner_swap(block, axis):
    count = lax.axis_size(axis)
    return lax.ppermute(block, axis, [(i, i ^ 1) for i in range(count)])


def outer_swap(block, axis):
    count = lax.axis_size(axis)
    partner = {i: i + 1 if i % 2 else i - 1 for i in range(count)}
    return lax.ppermute(block, axis, [(i, j) for i, j in partner.items() if 0 <= j < count])


def silu_parts(values):
    sigmoid_v = jax.nn.sigmoid(values)
    return values * sigmoid_v, sigmoid_v * (1.0 + values * (1.0 - sigmoid_v))


def mm(left, right):
    return lax.dot_general(left, right, (((1,), (0,)), ((), ())), preferred_element_type=F32)


def mm_rows(left, right):
    return lax.dot_general(left, right, (((0,), (0,)), ((), ())), preferred_element_type=F32)


def mm_cols(left, right):
    return lax.dot_general(left, right, (((1,), (1,)), ((), ())), preferred_element_type=F32)


def column(row):
    return jnp.transpose(jnp.broadcast_to(row, (8, row.shape[-1])))[:, :1]


def one_hot_cols(ids_column, width):
    lane_ids = lax.broadcasted_iota(jnp.int32, (ids_column.shape[0], width), 1)
    return (ids_column == lane_ids).astype(F32).astype(BF16)


def one_hot_rows(ids_row, height):
    row_ids = lax.broadcasted_iota(jnp.int32, (height, ids_row.shape[-1]), 0)
    return (ids_row == row_ids).astype(F32).astype(BF16)


def block_kernel(
    low_ref,
    mid_ref,
    high_ref,
    nodes_ref,
    top_ref,
    cot_ref,
    w_src_ref,
    w_dst_ref,
    w_msg_ref,
    w_top_ref,
    src_ref,
    dst_ref,
    band_ref,
    updated_ref,
    grads_ref,
    window_ref,
    ext,
    picked,
    hidden,
    pre_grad,
    act_grad,
    act_slope,
    msg_slope,
    dst_cols,
    w_src,
    w_dst,
    w_msg,
    w_top,
    nodes_own,
    top_own,
    cot_own,
    arrived,
):
    held = (w_src, w_dst, w_msg, w_top, nodes_own, top_own, cot_own)
    sources = (w_src_ref, w_dst_ref, w_msg_ref, w_top_ref, nodes_ref, top_ref, cot_ref)
    copies = [
        pltpu.make_async_copy(source, target, arrived.at[place])
        for place, (source, target) in enumerate(zip(sources, held))
    ]
    for place in (4, 0, 1, 2, 3, 5, 6):
        copies[place].start()
    slots = src_ref.shape[-1]
    block, features = nodes_own.shape
    third = low_ref.shape[0]
    ext[0:third, :] = low_ref[...]
    ext[third : 2 * third, :] = mid_ref[...]
    ext[2 * third :, :] = high_ref[...]
    src_col = column(src_ref[...])
    dst_col = column(dst_ref[...])
    dst_rows = one_hot_rows(dst_ref[...], block)
    inflow = jnp.zeros((block, features), F32)
    for start in range(0, slots, CHUNK):
        span = slice(start, start + CHUNK)
        gathered = mm(one_hot_cols(src_col[span], ext.shape[0]), ext[...]).astype(BF16)
        picked[span, :] = gathered
        if start == 0:
            for place in (4, 0, 1, 2):
                copies[place].wait()
            nodes = nodes_own[...]
        at_dst = one_hot_cols(dst_col[span], block)
        dst_cols[span, :] = at_dst
        local = mm(at_dst, nodes).astype(BF16)
        pre_act = mm(gathered, w_src[...]) + mm(local, w_dst[...])
        value, slope = silu_parts(pre_act)
        act_slope[span, :] = slope
        hid = value.astype(BF16)
        hidden[span, :] = hid
        value, slope = silu_parts(mm(hid, w_msg[...]))
        msg_slope[span, :] = slope
        inflow = inflow + mm(dst_rows[:, span], value.astype(BF16))
    for place in (3, 5, 6):
        copies[place].wait()
    top_count = top_own.shape[0]
    top_nodes = top_own[...]
    top_table = mm(top_nodes, w_top[...]).astype(BF16)
    band_col = column(band_ref[...])
    node_pre = inflow + mm(one_hot_cols(band_col, top_count), top_table)
    value, slope = silu_parts(node_pre)
    updated_ref[...] = (nodes.astype(F32) + value).astype(BF16)
    node_grad = (cot_own[...].astype(F32) * slope).astype(BF16)
    window = mm(one_hot_rows(band_ref[...], top_count), node_grad)
    window_ref[...] = window
    grads_ref[3] = mm_rows(top_nodes, window.astype(BF16)).astype(BF16)
    dst_grad = jnp.zeros((block, features), F32)
    for start in range(0, slots, CHUNK):
        span = slice(start, start + CHUNK)
        msg_grad = mm(dst_cols[span, :], node_grad)
        grad = (msg_grad * msg_slope[span, :]).astype(BF16)
        pre_grad[span, :] = grad
        grad = (mm_cols(grad, w_msg[...]) * act_slope[span, :]).astype(BF16)
        act_grad[span, :] = grad
        dst_grad = dst_grad + mm(dst_rows[:, span], grad)
    grads_ref[0] = mm_rows(picked[...], act_grad[...]).astype(BF16)
    grads_ref[1] = mm_rows(nodes, dst_grad.astype(BF16)).astype(BF16)
    grads_ref[2] = mm_rows(hidden[...], pre_grad[...]).astype(BF16)


def block_round(*args):
    nodes, top_nodes = args[3], args[4]
    slots = args[10].shape[-1]
    block, features = nodes.shape
    ext_rows = 3 * args[0].shape[0]
    hbm = pltpu.MemorySpace.HBM
    stay = [pltpu.with_memory_space_constraint(array, hbm) for array in args[3:10]]
    return pl.pallas_call(
        block_kernel,
        out_shape=(
            jax.ShapeDtypeStruct((block, features), BF16),
            jax.ShapeDtypeStruct((4, features, features), BF16),
            jax.ShapeDtypeStruct((top_nodes.shape[0], features), F32),
        ),
        scratch_shapes=[
            pltpu.VMEM((ext_rows, features), BF16),
            pltpu.VMEM((slots, features), BF16),
            pltpu.VMEM((slots, features), BF16),
            pltpu.VMEM((slots, features), BF16),
            pltpu.VMEM((slots, features), BF16),
            pltpu.VMEM((slots, features), F32),
            pltpu.VMEM((slots, features), F32),
            pltpu.VMEM((slots, block), BF16),
            pltpu.VMEM((features, features), BF16),
            pltpu.VMEM((features, features), BF16),
            pltpu.VMEM((features, features), BF16),
            pltpu.VMEM((features, features), BF16),
            pltpu.VMEM((block, features), BF16),
            pltpu.VMEM(top_nodes.shape, BF16),
            pltpu.VMEM((block, features), BF16),
            pltpu.SemaphoreType.DMA((7,)),
        ],
        in_specs=[pl.BlockSpec(memory_space=pltpu.MemorySpace.VMEM)] * 3
        + [pl.BlockSpec(memory_space=pltpu.MemorySpace.HBM)] * 7
        + [pl.BlockSpec(memory_space=pltpu.MemorySpace.VMEM)] * 3,
        compiler_params=pltpu.CompilerParams(vmem_limit_bytes=48 << 20),
        name="block_round",
    )(*args[:3], *stay, *args[10:])


def shards(
    nodes,
    top_nodes,
    cotangent,
    w_src,
    w_dst,
    w_msg,
    w_top,
    src_code,
    src_node,
    dst_node,
    edge_count,
    parent,
):
    block_size, features = nodes.shape[2:]
    slots = src_code.shape[-1]
    top_local = top_nodes.shape[0]
    owner_rows = top_local // lax.axis_size(LON)
    lon_index = lax.axis_index(LON)
    band_start = lax.axis_index(LAT) * top_local
    own = nodes.reshape(block_size, features)
    lat_odd, lon_odd = lax.axis_index("core"), lax.axis_index("x_lo")
    outer = outer_swap(own, LON)
    inner = inner_swap(own, LON)
    mid = jnp.concatenate([outer, own, inner], axis=0)
    low = outer_swap(mid, LAT)
    high = inner_swap(mid, LAT)
    src_row, src_col = src_code // 3, src_code % 3
    src_row = jnp.where(lat_odd == 1, 2 - src_row, src_row)
    src_col = jnp.where(lon_odd == 1, 2 - src_col, src_col)
    src_idx = ((src_row * 3 + src_col) * block_size + src_node).reshape(1, slots)
    live_slot = lax.broadcasted_iota(jnp.int32, (1, slots), 1) < edge_count
    dst_idx = jnp.where(live_slot, dst_node.reshape(1, slots), block_size)
    band_ids = parent.reshape(1, block_size) - band_start
    updated, grads, window = block_round(
        low,
        mid,
        high,
        own,
        top_nodes,
        cotangent.reshape(block_size, features),
        w_src,
        w_dst,
        w_msg,
        w_top,
        src_idx,
        dst_idx,
        band_ids,
    )
    nodes_total = block_size * lax.axis_size(LAT) * lax.axis_size(LON)
    grad_scale = 8.0 / math.sqrt(nodes_total)
    part = reduce_stage(grads.reshape(-1, features), CORE).astype(BF16)
    window, part = lax.optimization_barrier((window, part))
    padded = jnp.pad(window, ((owner_rows, owner_rows), (0, 0)))
    triple = lax.dynamic_slice_in_dim(padded, lon_index * owner_rows, 3 * owner_rows, 0)
    left, centre, right = jnp.split(triple, 3)
    from_inner = inner_swap(jnp.where(lon_odd == 1, left, right), LON)
    part = reduce_stage(part, NEAR).astype(BF16)
    part, from_inner = lax.optimization_barrier((part, from_inner))
    part = far_sum(part, grad_scale)
    part, left, right = lax.optimization_barrier((part, left, right))
    from_outer = outer_swap(jnp.where(lon_odd == 1, right, left), LON)
    part = gather_stage(part, NEAR)
    table_grad = (centre + from_inner + from_outer).astype(BF16)
    d_top = mm_cols(table_grad, w_top).astype(BF16)
    part, d_top = lax.optimization_barrier((part, d_top))
    weight_grads = gather_stage(part, CORE)
    return (
        updated.reshape(nodes.shape),
        weight_grads.reshape(4, features, features),
        d_top,
    )


def solution(mesh):
    lat_count, lon_count = mesh.shape["lat"], mesh.shape["lon"]
    fine = Mesh(
        mesh.devices.reshape(2, lat_count // 8, 2, 2, lon_count // 4, 2, 2),
        LAT + LON,
    )
    placed = (
        P(LAT, LON, None, None),
        P(LAT, None),
        P(LAT, LON, None, None),
        P(),
        P(),
        P(),
        P(),
        P(LAT, LON, None),
        P(LAT, LON, None),
        P(LAT, LON, None),
        P(LAT, LON),
        P(LAT, LON, None),
    )
    return jax.shard_map(
        shards,
        mesh=fine,
        in_specs=placed,
        out_specs=(P(LAT, LON, None, None), P(), P(LAT + LON, None)),
        check_vma=False,
    )
```

```python
import itertools
import math

import jax
import jax.numpy as jnp
from jax import lax
from jax.experimental import pallas as pl
from jax.experimental.pallas import tpu as pltpu
from jax.sharding import Mesh
from jax.sharding import PartitionSpec as P

LAT = ("x_hi", "z_hi", "z_lo", "core")
LON = ("y_hi", "y_lo", "x_lo")
AXES = LAT + LON
LANES = 128
CHUNK = 512
BF16 = jnp.bfloat16
F32 = jnp.float32


def member_groups():
    sizes = [lax.axis_size(name) for name in AXES]
    groups = ({}, {}, {})
    for device, place in enumerate(itertools.product(*map(range, sizes))):
        at = dict(zip(AXES, place))
        core = at["core"]
        chip = [2 * at[axis + "_hi"] + at[axis + "_lo"] for axis in "xyz"]
        counts = [2 * lax.axis_size(axis + "_hi") for axis in "xyz"]
        moved = [(spot + core) % count for spot, count in zip(chip, counts)]
        cube = tuple(spot // 2 for spot in moved)
        corner = tuple(spot % 2 for spot in moved)
        groups[0].setdefault(tuple(chip), []).append(device)
        groups[1].setdefault((core,) + cube, []).append((corner, device))
        groups[2].setdefault((core,) + corner, []).append((cube, device))
    pairs = list(groups[0].values())
    near, far = ([[device for _, device in sorted(g)] for g in d.values()] for d in groups[1:])
    return pairs, near, far


def exchange(part, groups):
    return lax.all_to_all(part, AXES, 0, 0, axis_index_groups=groups, tiled=True)


def reduce_stage(part, groups):
    got = exchange(part, groups)
    return jnp.sum(got.reshape(len(groups[0]), -1, got.shape[-1]).astype(F32), axis=0)


def gather_stage(part, groups):
    copies = jnp.broadcast_to(part[None], (len(groups[0]),) + part.shape)
    return exchange(copies.reshape(-1, part.shape[-1]), groups)


def lane_tiles(part):
    return jnp.concatenate(jnp.split(part, part.shape[1] // LANES, axis=1), axis=0)


def whole_rows(part, features):
    return jnp.concatenate(jnp.split(part, features // LANES, axis=0), axis=1)


def inner_swap(block, axis):
    count = lax.axis_size(axis)
    return lax.ppermute(block, axis, [(i, i ^ 1) for i in range(count)])


def outer_swap(block, axis):
    count = lax.axis_size(axis)
    partner = {i: i + 1 if i % 2 else i - 1 for i in range(count)}
    return lax.ppermute(block, axis, [(i, j) for i, j in partner.items() if 0 <= j < count])


def silu_parts(values):
    sigmoid_v = jax.nn.sigmoid(values)
    value = values * sigmoid_v
    return value, sigmoid_v + value * (1.0 - sigmoid_v)


def mm(left, right):
    return lax.dot_general(left, right, (((1,), (0,)), ((), ())), preferred_element_type=F32)


def mm_rows(left, right):
    return lax.dot_general(left, right, (((0,), (0,)), ((), ())), preferred_element_type=F32)


def mm_cols(left, right):
    return lax.dot_general(left, right, (((1,), (1,)), ((), ())), preferred_element_type=F32)


def column(row):
    return jnp.transpose(jnp.broadcast_to(row, (8, row.shape[-1])))[:, :1]


def one_hot_cols(ids_column, width):
    lane_ids = lax.broadcasted_iota(jnp.int32, (ids_column.shape[0], width), 1)
    return (ids_column == lane_ids).astype(F32).astype(BF16)


def one_hot_rows(ids_row, height):
    row_ids = lax.broadcasted_iota(jnp.int32, (height, ids_row.shape[-1]), 0)
    return (ids_row == row_ids).astype(F32).astype(BF16)


def block_kernel(
    low_ref,
    mid_ref,
    high_ref,
    nodes_ref,
    top_ref,
    cot_ref,
    w_src_ref,
    w_dst_ref,
    w_msg_ref,
    w_top_ref,
    src_ref,
    dst_ref,
    band_ref,
    updated_ref,
    grads_ref,
    window_ref,
    ext,
    picked,
    hidden,
    pre_grad,
    act_grad,
    act_slope,
    msg_slope,
    dst_cols,
    w_src,
    w_dst,
    w_msg,
    w_top,
    nodes_own,
    top_own,
    cot_own,
    arrived,
):
    held = (w_src, w_dst, w_msg, w_top, nodes_own, top_own, cot_own)
    sources = (w_src_ref, w_dst_ref, w_msg_ref, w_top_ref, nodes_ref, top_ref, cot_ref)
    copies = [
        pltpu.make_async_copy(source, target, arrived.at[place])
        for place, (source, target) in enumerate(zip(sources, held))
    ]
    for place in (4, 0, 1, 2, 3, 5, 6):
        copies[place].start()
    slots = src_ref.shape[-1]
    block, features = nodes_own.shape
    third = low_ref.shape[0]
    ext[0:third, :] = low_ref[...]
    ext[third : 2 * third, :] = mid_ref[...]
    ext[2 * third :, :] = high_ref[...]
    src_col = column(src_ref[...])
    dst_col = column(dst_ref[...])
    dst_rows = one_hot_rows(dst_ref[...], block)
    inflow = jnp.zeros((block, features), F32)
    for start in range(0, slots, CHUNK):
        span = slice(start, start + CHUNK)
        at_src = one_hot_cols(src_col[span], ext.shape[0])
        picked[span, :] = mm(at_src, ext[...]).astype(BF16)
        dst_cols[span, :] = one_hot_cols(dst_col[span], block)
    for place in (4, 0, 1):
        copies[place].wait()
    nodes = nodes_own[...]
    for start in range(0, slots, CHUNK):
        span = slice(start, start + CHUNK)
        local = mm(dst_cols[span, :], nodes).astype(BF16)
        pre_act = mm(picked[span, :], w_src[...]) + mm(local, w_dst[...])
        value, slope = silu_parts(pre_act)
        act_slope[span, :] = slope
        hidden[span, :] = value.astype(BF16)
    copies[2].wait()
    for start in range(0, slots, CHUNK):
        span = slice(start, start + CHUNK)
        value, slope = silu_parts(mm(hidden[span, :], w_msg[...]))
        msg_slope[span, :] = slope
        inflow = inflow + mm(dst_rows[:, span], value.astype(BF16))
    for place in (3, 5, 6):
        copies[place].wait()
    top_count = top_own.shape[0]
    top_nodes = top_own[...]
    top_table = mm(top_nodes, w_top[...]).astype(BF16)
    band_col = column(band_ref[...])
    node_pre = inflow + mm(one_hot_cols(band_col, top_count), top_table)
    value, slope = silu_parts(node_pre)
    updated_ref[...] = (nodes.astype(F32) + value).astype(BF16)
    node_grad = (cot_own[...].astype(F32) * slope).astype(BF16)
    window = mm(one_hot_rows(band_ref[...], top_count), node_grad)
    window_ref[...] = window
    grads_ref[3] = mm_rows(top_nodes, window.astype(BF16)).astype(BF16)
    dst_grad = jnp.zeros((block, features), F32)
    for start in range(0, slots, CHUNK):
        span = slice(start, start + CHUNK)
        msg_grad = mm(dst_cols[span, :], node_grad)
        grad = (msg_grad * msg_slope[span, :]).astype(BF16)
        pre_grad[span, :] = grad
        grad = (mm_cols(grad, w_msg[...]) * act_slope[span, :]).astype(BF16)
        act_grad[span, :] = grad
        dst_grad = dst_grad + mm(dst_rows[:, span], grad)
    grads_ref[0] = mm_rows(picked[...], act_grad[...]).astype(BF16)
    grads_ref[1] = mm_rows(nodes, dst_grad.astype(BF16)).astype(BF16)
    grads_ref[2] = mm_rows(hidden[...], pre_grad[...]).astype(BF16)


def block_round(*args):
    nodes, top_nodes = args[3], args[4]
    slots = args[10].shape[-1]
    block, features = nodes.shape
    ext_rows = 3 * args[0].shape[0]
    hbm = pltpu.MemorySpace.HBM
    stay = [pltpu.with_memory_space_constraint(array, hbm) for array in args[3:10]]
    return pl.pallas_call(
        block_kernel,
        out_shape=(
            jax.ShapeDtypeStruct((block, features), BF16),
            jax.ShapeDtypeStruct((4, features, features), BF16),
            jax.ShapeDtypeStruct((top_nodes.shape[0], features), F32),
        ),
        scratch_shapes=[
            pltpu.VMEM((ext_rows, features), BF16),
            pltpu.VMEM((slots, features), BF16),
            pltpu.VMEM((slots, features), BF16),
            pltpu.VMEM((slots, features), BF16),
            pltpu.VMEM((slots, features), BF16),
            pltpu.VMEM((slots, features), F32),
            pltpu.VMEM((slots, features), F32),
            pltpu.VMEM((slots, block), BF16),
            pltpu.VMEM((features, features), BF16),
            pltpu.VMEM((features, features), BF16),
            pltpu.VMEM((features, features), BF16),
            pltpu.VMEM((features, features), BF16),
            pltpu.VMEM((block, features), BF16),
            pltpu.VMEM(top_nodes.shape, BF16),
            pltpu.VMEM((block, features), BF16),
            pltpu.SemaphoreType.DMA((7,)),
        ],
        in_specs=[pl.BlockSpec(memory_space=pltpu.MemorySpace.VMEM)] * 3
        + [pl.BlockSpec(memory_space=pltpu.MemorySpace.HBM)] * 7
        + [pl.BlockSpec(memory_space=pltpu.MemorySpace.VMEM)] * 3,
        compiler_params=pltpu.CompilerParams(vmem_limit_bytes=48 << 20),
        name="block_round",
    )(*args[:3], *stay, *args[10:])


def shards(
    nodes,
    top_nodes,
    cotangent,
    w_src,
    w_dst,
    w_msg,
    w_top,
    src_code,
    src_node,
    dst_node,
    edge_count,
    parent,
):
    block_size, features = nodes.shape[2:]
    slots = src_code.shape[-1]
    top_local = top_nodes.shape[0]
    owner_rows = top_local // lax.axis_size(LON)
    lon_index = lax.axis_index(LON)
    band_start = lax.axis_index(LAT) * top_local
    own = nodes.reshape(block_size, features)
    lat_odd, lon_odd = lax.axis_index("core"), lax.axis_index("x_lo")
    outer = outer_swap(own, LON)
    inner = inner_swap(own, LON)
    mid = jnp.concatenate([outer, own, inner], axis=0)
    low = outer_swap(mid, LAT)
    high = inner_swap(mid, LAT)
    src_row, src_col = src_code // 3, src_code % 3
    src_row = jnp.where(lat_odd == 1, 2 - src_row, src_row)
    src_col = jnp.where(lon_odd == 1, 2 - src_col, src_col)
    src_idx = ((src_row * 3 + src_col) * block_size + src_node).reshape(1, slots)
    live_slot = lax.broadcasted_iota(jnp.int32, (1, slots), 1) < edge_count
    dst_idx = jnp.where(live_slot, dst_node.reshape(1, slots), block_size)
    band_ids = parent.reshape(1, block_size) - band_start
    updated, grads, window = block_round(
        low,
        mid,
        high,
        own,
        top_nodes,
        cotangent.reshape(block_size, features),
        w_src,
        w_dst,
        w_msg,
        w_top,
        src_idx,
        dst_idx,
        band_ids,
    )
    nodes_total = block_size * lax.axis_size(LAT) * lax.axis_size(LON)
    grad_scale = 8.0 / math.sqrt(nodes_total)
    pairs, near, far = member_groups()
    part = reduce_stage(grads.reshape(-1, features), pairs).astype(BF16)
    part = reduce_stage(part, near).astype(BF16)
    part = (reduce_stage(lane_tiles(part), far) * grad_scale).astype(BF16)
    window, part = lax.optimization_barrier((window, part))
    padded = jnp.pad(window, ((owner_rows, owner_rows), (0, 0)))
    triple = lax.dynamic_slice_in_dim(padded, lon_index * owner_rows, 3 * owner_rows, 0)
    left, centre, right = jnp.split(triple, 3)
    from_inner = inner_swap(jnp.where(lon_odd == 1, left, right), LON)
    from_outer = outer_swap(jnp.where(lon_odd == 1, right, left), LON)
    table_grad = (centre + from_inner + from_outer).astype(BF16)
    d_top = mm_cols(table_grad, w_top).astype(BF16)
    part = gather_stage(part, far)
    part, d_top = lax.optimization_barrier((part, d_top))
    part = gather_stage(whole_rows(part, features), near)
    weight_grads = gather_stage(part, pairs)
    return (
        updated.reshape(nodes.shape),
        weight_grads.reshape(4, features, features),
        d_top,
    )


def solution(mesh):
    lat_count, lon_count = mesh.shape["lat"], mesh.shape["lon"]
    fine = Mesh(
        mesh.devices.reshape(2, lat_count // 8, 2, 2, lon_count // 4, 2, 2),
        AXES,
    )
    placed = (
        P(LAT, LON, None, None),
        P(LAT, None),
        P(LAT, LON, None, None),
        P(),
        P(),
        P(),
        P(),
        P(LAT, LON, None),
        P(LAT, LON, None),
        P(LAT, LON, None),
        P(LAT, LON),
        P(LAT, LON, None),
    )
    return jax.shard_map(
        shards,
        mesh=fine,
        in_specs=placed,
        out_specs=(P(LAT, LON, None, None), P(), P(AXES, None)),
        check_vma=False,
    )
```

```python
import itertools
import math

import jax
import jax.numpy as jnp
from jax import lax
from jax.experimental import pallas as pl
from jax.experimental.pallas import tpu as pltpu
from jax.sharding import Mesh
from jax.sharding import PartitionSpec as P

LAT = ("x_hi", "z_hi", "z_lo", "core")
LON = ("y_hi", "y_lo", "x_lo")
AXES = LAT + LON
LANES = 128
CHUNK = 512
BF16 = jnp.bfloat16
F32 = jnp.float32


def member_groups():
    sizes = [lax.axis_size(name) for name in AXES]
    groups = ({}, {}, {})
    for device, place in enumerate(itertools.product(*map(range, sizes))):
        at = dict(zip(AXES, place))
        core = at["core"]
        chip = [2 * at[axis + "_hi"] + at[axis + "_lo"] for axis in "xyz"]
        counts = [2 * lax.axis_size(axis + "_hi") for axis in "xyz"]
        moved = [(spot + core) % count for spot, count in zip(chip, counts)]
        cube = tuple(spot // 2 for spot in moved)
        corner = tuple(spot % 2 for spot in moved)
        groups[0].setdefault(tuple(chip), []).append(device)
        groups[1].setdefault((core,) + cube, []).append((corner, device))
        groups[2].setdefault((core,) + corner, []).append((cube, device))
    pairs = list(groups[0].values())
    near, far = ([[device for _, device in sorted(g)] for g in d.values()] for d in groups[1:])
    return pairs, near, far


def exchange(part, groups):
    return lax.all_to_all(part, AXES, 0, 0, axis_index_groups=groups, tiled=True)


def reduce_stage(part, groups):
    got = exchange(part, groups)
    return jnp.sum(got.reshape(len(groups[0]), -1, got.shape[-1]).astype(F32), axis=0)


def gather_stage(part, groups):
    copies = jnp.broadcast_to(part[None], (len(groups[0]),) + part.shape)
    return exchange(copies.reshape(-1, part.shape[-1]), groups)


def lane_tiles(part):
    return jnp.concatenate(jnp.split(part, part.shape[1] // LANES, axis=1), axis=0)


def whole_rows(part, features):
    return jnp.concatenate(jnp.split(part, features // LANES, axis=0), axis=1)


def inner_swap(block, axis):
    count = lax.axis_size(axis)
    return lax.ppermute(block, axis, [(i, i ^ 1) for i in range(count)])


def outer_swap(block, axis):
    count = lax.axis_size(axis)
    partner = {i: i + 1 if i % 2 else i - 1 for i in range(count)}
    return lax.ppermute(block, axis, [(i, j) for i, j in partner.items() if 0 <= j < count])


def silu_parts(values):
    sigmoid_v = jax.nn.sigmoid(values)
    value = values * sigmoid_v
    return value, sigmoid_v + value * (1.0 - sigmoid_v)


def mm(left, right):
    return lax.dot_general(left, right, (((1,), (0,)), ((), ())), preferred_element_type=F32)


def mm_rows(left, right):
    return lax.dot_general(left, right, (((0,), (0,)), ((), ())), preferred_element_type=F32)


def mm_cols(left, right):
    return lax.dot_general(left, right, (((1,), (1,)), ((), ())), preferred_element_type=F32)


def column(row):
    return jnp.transpose(jnp.broadcast_to(row, (8, row.shape[-1])))[:, :1]


def one_hot_cols(ids_column, width):
    lane_ids = lax.broadcasted_iota(jnp.int32, (ids_column.shape[0], width), 1)
    return (ids_column == lane_ids).astype(F32).astype(BF16)


def one_hot_rows(ids_row, height):
    row_ids = lax.broadcasted_iota(jnp.int32, (height, ids_row.shape[-1]), 0)
    return (ids_row == row_ids).astype(F32).astype(BF16)


def first_kernel(
    mid_ref,
    top_ref,
    cot_ref,
    w_src_ref,
    w_dst_ref,
    w_msg_ref,
    w_top_ref,
    src_ref,
    dst_ref,
    band_ref,
    picked_ref,
    dst_pre_ref,
    rows_ref,
    dst_cols_ref,
    top_own,
    cot_own,
    w_src,
    w_msg,
    w_dst,
    w_top,
    arrived,
):
    moves = (
        (w_dst_ref, w_dst),
        (w_top_ref, w_top),
        (top_ref, top_own),
        (w_src_ref, w_src),
        (w_msg_ref, w_msg),
        (cot_ref, cot_own),
    )
    copies = [
        pltpu.make_async_copy(source, target, arrived.at[place])
        for place, (source, target) in enumerate(moves)
    ]
    for copy in copies:
        copy.start()
    slots = src_ref.shape[-1]
    third = mid_ref.shape[0]
    block = third // 3
    nodes = mid_ref[block : 2 * block, :]
    src_col = column(src_ref[...]) - third
    dst_col = column(dst_ref[...])
    for start in range(0, slots, CHUNK):
        span = slice(start, start + CHUNK)
        at_src = one_hot_cols(src_col[span], third)
        picked_ref[span, :] = mm(at_src, mid_ref[...]).astype(BF16)
        dst_cols_ref[span, :] = one_hot_cols(dst_col[span], block)
    copies[0].wait()
    for start in range(0, slots, CHUNK):
        span = slice(start, start + CHUNK)
        local = mm(dst_cols_ref[span, :], nodes).astype(BF16)
        dst_pre_ref[span, :] = mm(local, w_dst[...])
    copies[1].wait()
    copies[2].wait()
    top_table = mm(top_own[...], w_top[...]).astype(BF16)
    band_col = column(band_ref[...])
    rows_ref[...] = mm(one_hot_cols(band_col, top_own.shape[0]), top_table)
    for copy in copies[3:]:
        copy.wait()


def first_round(mid, *args):
    top_nodes, cot, w_src = args[0], args[1], args[2]
    slots = args[6].shape[-1]
    block, features = cot.shape
    vmem = pl.BlockSpec(memory_space=pltpu.MemorySpace.VMEM)
    hbm = pltpu.MemorySpace.HBM
    stay = [pltpu.with_memory_space_constraint(array, hbm) for array in args[:6]]
    return pl.pallas_call(
        first_kernel,
        out_shape=(
            jax.ShapeDtypeStruct((slots, features), BF16),
            jax.ShapeDtypeStruct((slots, features), F32),
            jax.ShapeDtypeStruct((block, features), F32),
            jax.ShapeDtypeStruct((slots, block), BF16),
            jax.ShapeDtypeStruct(top_nodes.shape, BF16),
            jax.ShapeDtypeStruct(cot.shape, BF16),
            jax.ShapeDtypeStruct(w_src.shape, BF16),
            jax.ShapeDtypeStruct(w_src.shape, BF16),
        ),
        scratch_shapes=[
            pltpu.VMEM(w_src.shape, BF16),
            pltpu.VMEM(w_src.shape, BF16),
            pltpu.SemaphoreType.DMA((6,)),
        ],
        in_specs=[vmem] + [pl.BlockSpec(memory_space=hbm)] * 6 + [vmem] * 3,
        out_specs=(vmem,) * 8,
        compiler_params=pltpu.CompilerParams(vmem_limit_bytes=32 << 20),
        name="first_round",
    )(mid, *stay, *args[6:])


def block_kernel(
    low_ref,
    mid_ref,
    high_ref,
    src_ref,
    dst_ref,
    band_ref,
    picked_ref,
    dst_pre_ref,
    rows_ref,
    dst_cols,
    top_ref,
    cot_ref,
    w_src,
    w_msg,
    updated_ref,
    grads_ref,
    window_ref,
    ext,
    picked,
    hidden,
    pre_grad,
    act_grad,
    act_slope,
    msg_slope,
):
    slots = src_ref.shape[-1]
    third, features = mid_ref.shape
    block = third // 3
    ext[0:third, :] = low_ref[...]
    ext[third:, :] = high_ref[...]
    nodes = mid_ref[block : 2 * block, :]
    src_row = src_ref[...]
    src_row = jnp.where(src_row < third, src_row, src_row - third)
    inside = (src_ref[...] >= third) & (src_ref[...] < 2 * third)
    src_col = column(jnp.where(inside, -1, src_row))
    dst_rows = one_hot_rows(dst_ref[...], block)
    inflow = rows_ref[...]
    for start in range(0, slots, CHUNK):
        span = slice(start, start + CHUNK)
        other = mm(one_hot_cols(src_col[span], 2 * third), ext[...])
        gathered = (other + picked_ref[span, :].astype(F32)).astype(BF16)
        picked[span, :] = gathered
        pre_act = mm(gathered, w_src[...]) + dst_pre_ref[span, :]
        value, slope = silu_parts(pre_act)
        act_slope[span, :] = slope
        hid = value.astype(BF16)
        hidden[span, :] = hid
        value, slope = silu_parts(mm(hid, w_msg[...]))
        msg_slope[span, :] = slope
        inflow = inflow + mm(dst_rows[:, span], value.astype(BF16))
    value, slope = silu_parts(inflow)
    updated_ref[...] = (nodes.astype(F32) + value).astype(BF16)
    node_grad = (cot_ref[...].astype(F32) * slope).astype(BF16)
    top_nodes = top_ref[...]
    window = mm(one_hot_rows(band_ref[...], top_nodes.shape[0]), node_grad)
    window_ref[...] = window
    grads_ref[3] = mm_rows(top_nodes, window.astype(BF16)).astype(BF16)
    dst_grad = jnp.zeros((block, features), F32)
    for start in range(0, slots, CHUNK):
        span = slice(start, start + CHUNK)
        msg_grad = mm(dst_cols[span, :], node_grad)
        grad = (msg_grad * msg_slope[span, :]).astype(BF16)
        pre_grad[span, :] = grad
        grad = (mm_cols(grad, w_msg[...]) * act_slope[span, :]).astype(BF16)
        act_grad[span, :] = grad
        dst_grad = dst_grad + mm(dst_rows[:, span], grad)
    grads_ref[0] = mm_rows(picked[...], act_grad[...]).astype(BF16)
    grads_ref[1] = mm_rows(nodes, dst_grad.astype(BF16)).astype(BF16)
    grads_ref[2] = mm_rows(hidden[...], pre_grad[...]).astype(BF16)


def block_round(low, mid, high, src_idx, *rest):
    slots = src_idx.shape[-1]
    third, features = mid.shape
    top_rows = rest[6].shape[0]
    vmem = pl.BlockSpec(memory_space=pltpu.MemorySpace.VMEM)
    return pl.pallas_call(
        block_kernel,
        out_shape=(
            jax.ShapeDtypeStruct((third // 3, features), BF16),
            jax.ShapeDtypeStruct((4, features, features), BF16),
            jax.ShapeDtypeStruct((top_rows, features), F32),
        ),
        scratch_shapes=[pltpu.VMEM((2 * third, features), BF16)]
        + [pltpu.VMEM((slots, features), BF16)] * 4
        + [pltpu.VMEM((slots, features), F32)] * 2,
        in_specs=[vmem] * (4 + len(rest)),
        out_specs=(vmem,) * 3,
        compiler_params=pltpu.CompilerParams(vmem_limit_bytes=40 << 20),
        name="block_round",
    )(low, mid, high, src_idx, *rest)


def shards(
    nodes,
    top_nodes,
    cotangent,
    w_src,
    w_dst,
    w_msg,
    w_top,
    src_code,
    src_node,
    dst_node,
    edge_count,
    parent,
):
    block_size, features = nodes.shape[2:]
    slots = src_code.shape[-1]
    top_local = top_nodes.shape[0]
    owner_rows = top_local // lax.axis_size(LON)
    lon_index = lax.axis_index(LON)
    band_start = lax.axis_index(LAT) * top_local
    own = nodes.reshape(block_size, features)
    lat_odd, lon_odd = lax.axis_index("core"), lax.axis_index("x_lo")
    outer = outer_swap(own, LON)
    inner = inner_swap(own, LON)
    mid = jnp.concatenate([outer, own, inner], axis=0)
    low = outer_swap(mid, LAT)
    high = inner_swap(mid, LAT)
    src_row, src_col = src_code // 3, src_code % 3
    src_row = jnp.where(lat_odd == 1, 2 - src_row, src_row)
    src_col = jnp.where(lon_odd == 1, 2 - src_col, src_col)
    src_idx = ((src_row * 3 + src_col) * block_size + src_node).reshape(1, slots)
    live_slot = lax.broadcasted_iota(jnp.int32, (1, slots), 1) < edge_count
    dst_idx = jnp.where(live_slot, dst_node.reshape(1, slots), block_size)
    band_ids = parent.reshape(1, block_size) - band_start
    ready = first_round(
        mid,
        top_nodes,
        cotangent.reshape(block_size, features),
        w_src,
        w_dst,
        w_msg,
        w_top,
        src_idx,
        dst_idx,
        band_ids,
    )
    updated, grads, window = block_round(
        low, mid, high, src_idx, dst_idx, band_ids, *ready
    )
    nodes_total = block_size * lax.axis_size(LAT) * lax.axis_size(LON)
    grad_scale = 8.0 / math.sqrt(nodes_total)
    pairs, near, far = member_groups()
    part = reduce_stage(grads.reshape(-1, features), pairs).astype(BF16)
    part = reduce_stage(part, near).astype(BF16)
    part = (reduce_stage(lane_tiles(part), far) * grad_scale).astype(BF16)
    window, part = lax.optimization_barrier((window, part))
    padded = jnp.pad(window, ((owner_rows, owner_rows), (0, 0)))
    triple = lax.dynamic_slice_in_dim(padded, lon_index * owner_rows, 3 * owner_rows, 0)
    left, centre, right = jnp.split(triple, 3)
    from_inner = inner_swap(jnp.where(lon_odd == 1, left, right), LON)
    from_outer = outer_swap(jnp.where(lon_odd == 1, right, left), LON)
    table_grad = (centre + from_inner + from_outer).astype(BF16)
    d_top = mm_cols(table_grad, w_top).astype(BF16)
    part = gather_stage(part, far)
    part, d_top = lax.optimization_barrier((part, d_top))
    part = gather_stage(whole_rows(part, features), near)
    weight_grads = gather_stage(part, pairs)
    return (
        updated.reshape(nodes.shape),
        weight_grads.reshape(4, features, features),
        d_top,
    )


def solution(mesh):
    lat_count, lon_count = mesh.shape["lat"], mesh.shape["lon"]
    fine = Mesh(
        mesh.devices.reshape(2, lat_count // 8, 2, 2, lon_count // 4, 2, 2),
        AXES,
    )
    placed = (
        P(LAT, LON, None, None),
        P(LAT, None),
        P(LAT, LON, None, None),
        P(),
        P(),
        P(),
        P(),
        P(LAT, LON, None),
        P(LAT, LON, None),
        P(LAT, LON, None),
        P(LAT, LON),
        P(LAT, LON, None),
    )
    return jax.shard_map(
        shards,
        mesh=fine,
        in_specs=placed,
        out_specs=(P(LAT, LON, None, None), P(), P(AXES, None)),
        check_vma=False,
    )
```

```python
import itertools
import math

import jax
import jax.numpy as jnp
from jax import lax
from jax.experimental import pallas as pl
from jax.experimental.pallas import tpu as pltpu
from jax.sharding import Mesh
from jax.sharding import PartitionSpec as P

LAT = ("x_hi", "z_hi", "z_lo", "core")
LON = ("y_hi", "y_lo", "x_lo")
AXES = LAT + LON
CHUNK = 512
BF16 = jnp.bfloat16
F32 = jnp.float32


def member_groups():
    sizes = [lax.axis_size(name) for name in AXES]
    counts = [2 * lax.axis_size(axis + "_hi") for axis in "xyz"]
    groups = ({}, {}, {}, {})
    for device, place in enumerate(itertools.product(*map(range, sizes))):
        at = dict(zip(AXES, place))
        core = at["core"]
        chip = tuple(2 * at[axis + "_hi"] + at[axis + "_lo"] for axis in "xyz")
        moved = [(spot + core) % count for spot, count in zip(chip, counts)]
        cube = tuple(spot // 2 for spot in moved)
        corner = tuple(spot % 2 for spot in moved)
        keys = (chip, (core, cube), (core, corner, cube[2]), (core, corner, cube[:2]))
        spots = (core, corner, cube[:2], cube[2])
        for kind, key, spot in zip(groups, keys, spots):
            kind.setdefault(key, []).append((spot, device))
    return [[[device for _, device in sorted(g)] for g in kind.values()] for kind in groups]


def exchange(part, groups):
    return lax.all_to_all(part, AXES, 0, 0, axis_index_groups=groups, tiled=True)


def reduce_stage(part, groups):
    got = exchange(part, groups)
    return jnp.sum(got.reshape(len(groups[0]), -1, got.shape[-1]).astype(F32), axis=0)


def gather_stage(part, groups):
    copies = jnp.broadcast_to(part[None], (len(groups[0]),) + part.shape)
    return exchange(copies.reshape(-1, part.shape[-1]), groups)


def inner_swap(block, axis):
    count = lax.axis_size(axis)
    return lax.ppermute(block, axis, [(i, i ^ 1) for i in range(count)])


def outer_swap(block, axis):
    count = lax.axis_size(axis)
    partner = {i: i + 1 if i % 2 else i - 1 for i in range(count)}
    return lax.ppermute(block, axis, [(i, j) for i, j in partner.items() if 0 <= j < count])


def silu_parts(values):
    sigmoid_v = jax.nn.sigmoid(values)
    value = values * sigmoid_v
    return value, sigmoid_v + value * (1.0 - sigmoid_v)


def mm(left, right):
    return lax.dot_general(left, right, (((1,), (0,)), ((), ())), preferred_element_type=F32)


def mm_rows(left, right):
    return lax.dot_general(left, right, (((0,), (0,)), ((), ())), preferred_element_type=F32)


def mm_cols(left, right):
    return lax.dot_general(left, right, (((1,), (1,)), ((), ())), preferred_element_type=F32)


def column(row):
    return jnp.transpose(jnp.broadcast_to(row, (8, row.shape[-1])))[:, :1]


def one_hot_cols(ids_column, width):
    lane_ids = lax.broadcasted_iota(jnp.int32, (ids_column.shape[0], width), 1)
    return (ids_column == lane_ids).astype(F32).astype(BF16)


def one_hot_rows(ids_row, height):
    row_ids = lax.broadcasted_iota(jnp.int32, (height, ids_row.shape[-1]), 0)
    return (ids_row == row_ids).astype(F32).astype(BF16)


def first_kernel(
    mid_ref,
    top_ref,
    cot_ref,
    w_src_ref,
    w_dst_ref,
    w_msg_ref,
    w_top_ref,
    src_ref,
    dst_ref,
    band_ref,
    picked_ref,
    dst_pre_ref,
    rows_ref,
    dst_cols_ref,
    top_own,
    cot_own,
    w_src,
    w_msg,
    w_dst,
    w_top,
    arrived,
):
    moves = (
        (w_dst_ref, w_dst),
        (w_top_ref, w_top),
        (top_ref, top_own),
        (w_src_ref, w_src),
        (w_msg_ref, w_msg),
        (cot_ref, cot_own),
    )
    copies = [
        pltpu.make_async_copy(source, target, arrived.at[place])
        for place, (source, target) in enumerate(moves)
    ]
    for copy in copies:
        copy.start()
    slots = src_ref.shape[-1]
    third = mid_ref.shape[0]
    block = third // 3
    nodes = mid_ref[block : 2 * block, :]
    src_col = column(src_ref[...]) - third
    dst_col = column(dst_ref[...])
    for start in range(0, slots, CHUNK):
        span = slice(start, start + CHUNK)
        at_src = one_hot_cols(src_col[span], third)
        picked_ref[span, :] = mm(at_src, mid_ref[...]).astype(BF16)
        dst_cols_ref[span, :] = one_hot_cols(dst_col[span], block)
    copies[0].wait()
    for start in range(0, slots, CHUNK):
        span = slice(start, start + CHUNK)
        local = mm(dst_cols_ref[span, :], nodes).astype(BF16)
        dst_pre_ref[span, :] = mm(local, w_dst[...])
    copies[1].wait()
    copies[2].wait()
    top_table = mm(top_own[...], w_top[...]).astype(BF16)
    band_col = column(band_ref[...])
    rows_ref[...] = mm(one_hot_cols(band_col, top_own.shape[0]), top_table)
    for copy in copies[3:]:
        copy.wait()


def first_round(mid, *args):
    top_nodes, cot, w_src = args[0], args[1], args[2]
    slots = args[6].shape[-1]
    block, features = cot.shape
    vmem = pl.BlockSpec(memory_space=pltpu.MemorySpace.VMEM)
    hbm = pltpu.MemorySpace.HBM
    stay = [pltpu.with_memory_space_constraint(array, hbm) for array in args[:6]]
    return pl.pallas_call(
        first_kernel,
        out_shape=(
            jax.ShapeDtypeStruct((slots, features), BF16),
            jax.ShapeDtypeStruct((slots, features), F32),
            jax.ShapeDtypeStruct((block, features), F32),
            jax.ShapeDtypeStruct((slots, block), BF16),
            jax.ShapeDtypeStruct(top_nodes.shape, BF16),
            jax.ShapeDtypeStruct(cot.shape, BF16),
            jax.ShapeDtypeStruct(w_src.shape, BF16),
            jax.ShapeDtypeStruct(w_src.shape, BF16),
        ),
        scratch_shapes=[
            pltpu.VMEM(w_src.shape, BF16),
            pltpu.VMEM(w_src.shape, BF16),
            pltpu.SemaphoreType.DMA((6,)),
        ],
        in_specs=[vmem] + [pl.BlockSpec(memory_space=hbm)] * 6 + [vmem] * 3,
        out_specs=(vmem,) * 8,
        compiler_params=pltpu.CompilerParams(vmem_limit_bytes=32 << 20),
        name="first_round",
    )(mid, *stay, *args[6:])


def block_kernel(
    low_ref,
    mid_ref,
    high_ref,
    src_ref,
    dst_ref,
    band_ref,
    picked_ref,
    dst_pre_ref,
    rows_ref,
    dst_cols,
    top_ref,
    cot_ref,
    w_src,
    w_msg,
    updated_ref,
    grads_ref,
    window_ref,
    ext,
    picked,
    hidden,
    pre_grad,
    act_grad,
    act_slope,
    msg_slope,
):
    slots = src_ref.shape[-1]
    third, features = mid_ref.shape
    block = third // 3
    ext[0:third, :] = low_ref[...]
    ext[third:, :] = high_ref[...]
    nodes = mid_ref[block : 2 * block, :]
    src_row = src_ref[...]
    src_row = jnp.where(src_row < third, src_row, src_row - third)
    inside = (src_ref[...] >= third) & (src_ref[...] < 2 * third)
    src_col = column(jnp.where(inside, -1, src_row))
    dst_rows = one_hot_rows(dst_ref[...], block)
    inflow = rows_ref[...]
    for start in range(0, slots, CHUNK):
        span = slice(start, start + CHUNK)
        other = mm(one_hot_cols(src_col[span], 2 * third), ext[...])
        gathered = (other + picked_ref[span, :].astype(F32)).astype(BF16)
        picked[span, :] = gathered
        pre_act = mm(gathered, w_src[...]) + dst_pre_ref[span, :]
        value, slope = silu_parts(pre_act)
        act_slope[span, :] = slope
        hid = value.astype(BF16)
        hidden[span, :] = hid
        value, slope = silu_parts(mm(hid, w_msg[...]))
        msg_slope[span, :] = slope
        inflow = inflow + mm(dst_rows[:, span], value.astype(BF16))
    value, slope = silu_parts(inflow)
    updated_ref[...] = (nodes.astype(F32) + value).astype(BF16)
    node_grad = (cot_ref[...].astype(F32) * slope).astype(BF16)
    top_nodes = top_ref[...]
    window = mm(one_hot_rows(band_ref[...], top_nodes.shape[0]), node_grad)
    window_ref[...] = window
    grads_ref[3] = mm_rows(top_nodes, window.astype(BF16)).astype(BF16)
    dst_grad = jnp.zeros((block, features), F32)
    for start in range(0, slots, CHUNK):
        span = slice(start, start + CHUNK)
        msg_grad = mm(dst_cols[span, :], node_grad)
        grad = (msg_grad * msg_slope[span, :]).astype(BF16)
        pre_grad[span, :] = grad
        grad = (mm_cols(grad, w_msg[...]) * act_slope[span, :]).astype(BF16)
        act_grad[span, :] = grad
        dst_grad = dst_grad + mm(dst_rows[:, span], grad)
    grads_ref[0] = mm_rows(picked[...], act_grad[...]).astype(BF16)
    grads_ref[1] = mm_rows(nodes, dst_grad.astype(BF16)).astype(BF16)
    grads_ref[2] = mm_rows(hidden[...], pre_grad[...]).astype(BF16)


def block_round(low, mid, high, src_idx, *rest):
    slots = src_idx.shape[-1]
    third, features = mid.shape
    top_rows = rest[6].shape[0]
    vmem = pl.BlockSpec(memory_space=pltpu.MemorySpace.VMEM)
    return pl.pallas_call(
        block_kernel,
        out_shape=(
            jax.ShapeDtypeStruct((third // 3, features), BF16),
            jax.ShapeDtypeStruct((4, features, features), BF16),
            jax.ShapeDtypeStruct((top_rows, features), F32),
        ),
        scratch_shapes=[pltpu.VMEM((2 * third, features), BF16)]
        + [pltpu.VMEM((slots, features), BF16)] * 4
        + [pltpu.VMEM((slots, features), F32)] * 2,
        in_specs=[vmem] * (4 + len(rest)),
        out_specs=(vmem,) * 3,
        compiler_params=pltpu.CompilerParams(vmem_limit_bytes=40 << 20),
        name="block_round",
    )(low, mid, high, src_idx, *rest)


def shards(
    nodes,
    top_nodes,
    cotangent,
    w_src,
    w_dst,
    w_msg,
    w_top,
    src_code,
    src_node,
    dst_node,
    edge_count,
    parent,
):
    block_size, features = nodes.shape[2:]
    slots = src_code.shape[-1]
    top_local = top_nodes.shape[0]
    owner_rows = top_local // lax.axis_size(LON)
    lon_index = lax.axis_index(LON)
    band_start = lax.axis_index(LAT) * top_local
    own = nodes.reshape(block_size, features)
    lat_odd, lon_odd = lax.axis_index("core"), lax.axis_index("x_lo")
    outer = outer_swap(own, LON)
    inner = inner_swap(own, LON)
    mid = jnp.concatenate([outer, own, inner], axis=0)
    low = outer_swap(mid, LAT)
    high = inner_swap(mid, LAT)
    src_row, src_col = src_code // 3, src_code % 3
    src_row = jnp.where(lat_odd == 1, 2 - src_row, src_row)
    src_col = jnp.where(lon_odd == 1, 2 - src_col, src_col)
    src_idx = ((src_row * 3 + src_col) * block_size + src_node).reshape(1, slots)
    live_slot = lax.broadcasted_iota(jnp.int32, (1, slots), 1) < edge_count
    dst_idx = jnp.where(live_slot, dst_node.reshape(1, slots), block_size)
    band_ids = parent.reshape(1, block_size) - band_start
    ready = first_round(
        mid,
        top_nodes,
        cotangent.reshape(block_size, features),
        w_src,
        w_dst,
        w_msg,
        w_top,
        src_idx,
        dst_idx,
        band_ids,
    )
    updated, grads, window = block_round(
        low, mid, high, src_idx, dst_idx, band_ids, *ready
    )
    nodes_total = block_size * lax.axis_size(LAT) * lax.axis_size(LON)
    grad_scale = 8.0 / math.sqrt(nodes_total)
    pairs, near, flat, tall = member_groups()
    part = reduce_stage(grads.reshape(-1, features), pairs).astype(BF16)
    part = reduce_stage(part, near).astype(BF16)
    window, part = lax.optimization_barrier((window, part))
    padded = jnp.pad(window, ((owner_rows, owner_rows), (0, 0)))
    triple = lax.dynamic_slice_in_dim(padded, lon_index * owner_rows, 3 * owner_rows, 0)
    left, centre, right = jnp.split(triple, 3)
    from_inner = inner_swap(jnp.where(lon_odd == 1, left, right), LON)
    part = reduce_stage(part, flat)
    part, from_inner = lax.optimization_barrier((part, from_inner))
    every = gather_stage(part, tall).reshape((-1,) + part.shape)
    part = (jnp.sum(every, axis=0) * grad_scale).astype(BF16)
    part, left, right = lax.optimization_barrier((part, left, right))
    from_outer = outer_swap(jnp.where(lon_odd == 1, right, left), LON)
    table_grad = (centre + from_inner + from_outer).astype(BF16)
    d_top = mm_cols(table_grad, w_top).astype(BF16)
    part = gather_stage(part, flat)
    part, d_top = lax.optimization_barrier((part, d_top))
    part = gather_stage(part, near)
    weight_grads = gather_stage(part, pairs)
    return (
        updated.reshape(nodes.shape),
        weight_grads.reshape(4, features, features),
        d_top,
    )


def solution(mesh):
    lat_count, lon_count = mesh.shape["lat"], mesh.shape["lon"]
    fine = Mesh(
        mesh.devices.reshape(2, lat_count // 8, 2, 2, lon_count // 4, 2, 2),
        AXES,
    )
    placed = (
        P(LAT, LON, None, None),
        P(LAT, None),
        P(LAT, LON, None, None),
        P(),
        P(),
        P(),
        P(),
        P(LAT, LON, None),
        P(LAT, LON, None),
        P(LAT, LON, None),
        P(LAT, LON),
        P(LAT, LON, None),
    )
    return jax.shard_map(
        shards,
        mesh=fine,
        in_specs=placed,
        out_specs=(P(LAT, LON, None, None), P(), P(AXES, None)),
        check_vma=False,
    )
```

```python
import itertools
import math

import jax
import jax.numpy as jnp
from jax import lax
from jax.experimental import pallas as pl
from jax.experimental.pallas import tpu as pltpu
from jax.sharding import Mesh
from jax.sharding import PartitionSpec as P

LAT = ("x_hi", "z_hi", "z_lo", "core")
LON = ("y_hi", "y_lo", "x_lo")
AXES = LAT + LON
LANES = 128
CHUNK = 512
BF16 = jnp.bfloat16
F32 = jnp.float32


def member_groups():
    sizes = [lax.axis_size(name) for name in AXES]
    groups = ({}, {}, {})
    for device, place in enumerate(itertools.product(*map(range, sizes))):
        at = dict(zip(AXES, place))
        core = at["core"]
        chip = [2 * at[axis + "_hi"] + at[axis + "_lo"] for axis in "xyz"]
        counts = [2 * lax.axis_size(axis + "_hi") for axis in "xyz"]
        moved = [(spot + core) % count for spot, count in zip(chip, counts)]
        cube = tuple(spot // 2 for spot in moved)
        corner = tuple(spot % 2 for spot in moved)
        groups[0].setdefault(tuple(chip), []).append(device)
        groups[1].setdefault((core,) + cube, []).append((corner, device))
        groups[2].setdefault((core,) + corner, []).append((cube, device))
    pairs = list(groups[0].values())
    near, far = ([[device for _, device in sorted(g)] for g in d.values()] for d in groups[1:])
    return pairs, near, far


def exchange(part, groups):
    return lax.all_to_all(part, AXES, 0, 0, axis_index_groups=groups, tiled=True)


def reduce_stage(part, groups):
    got = exchange(part, groups)
    return jnp.sum(got.reshape(len(groups[0]), -1, got.shape[-1]).astype(F32), axis=0)


def copies_for(part, groups):
    copies = jnp.broadcast_to(part[None], (len(groups[0]),) + part.shape)
    return copies.reshape(-1, part.shape[-1])


def gather_stage(part, groups):
    return exchange(copies_for(part, groups), groups)


def lane_tiles(part):
    return jnp.concatenate(jnp.split(part, part.shape[1] // LANES, axis=1), axis=0)


def whole_rows(part, features):
    return jnp.concatenate(jnp.split(part, features // LANES, axis=0), axis=1)


def inner_swap(block, axis):
    count = lax.axis_size(axis)
    return lax.ppermute(block, axis, [(i, i ^ 1) for i in range(count)])


def outer_swap(block, axis):
    count = lax.axis_size(axis)
    partner = {i: i + 1 if i % 2 else i - 1 for i in range(count)}
    return lax.ppermute(block, axis, [(i, j) for i, j in partner.items() if 0 <= j < count])


def silu_parts(values):
    sigmoid_v = jax.nn.sigmoid(values)
    value = values * sigmoid_v
    return value, sigmoid_v + value * (1.0 - sigmoid_v)


def mm(left, right):
    return lax.dot_general(left, right, (((1,), (0,)), ((), ())), preferred_element_type=F32)


def mm_rows(left, right):
    return lax.dot_general(left, right, (((0,), (0,)), ((), ())), preferred_element_type=F32)


def mm_cols(left, right):
    return lax.dot_general(left, right, (((1,), (1,)), ((), ())), preferred_element_type=F32)


def column(row):
    return jnp.transpose(jnp.broadcast_to(row, (8, row.shape[-1])))[:, :1]


def one_hot_cols(ids_column, width):
    lane_ids = lax.broadcasted_iota(jnp.int32, (ids_column.shape[0], width), 1)
    return (ids_column == lane_ids).astype(F32).astype(BF16)


def one_hot_rows(ids_row, height):
    row_ids = lax.broadcasted_iota(jnp.int32, (height, ids_row.shape[-1]), 0)
    return (ids_row == row_ids).astype(F32).astype(BF16)


def first_kernel(
    mid_ref,
    top_ref,
    cot_ref,
    w_src_ref,
    w_dst_ref,
    w_msg_ref,
    w_top_ref,
    src_ref,
    dst_ref,
    band_ref,
    picked_ref,
    dst_pre_ref,
    rows_ref,
    dst_cols_ref,
    top_own,
    cot_own,
    w_src,
    w_msg,
    w_dst,
    w_top,
    arrived,
):
    moves = (
        (w_dst_ref, w_dst),
        (w_top_ref, w_top),
        (top_ref, top_own),
        (w_src_ref, w_src),
        (w_msg_ref, w_msg),
        (cot_ref, cot_own),
    )
    copies = [
        pltpu.make_async_copy(source, target, arrived.at[place])
        for place, (source, target) in enumerate(moves)
    ]
    for copy in copies:
        copy.start()
    slots = src_ref.shape[-1]
    third = mid_ref.shape[0]
    block = third // 3
    nodes = mid_ref[block : 2 * block, :]
    src_col = column(src_ref[...]) - third
    dst_col = column(dst_ref[...])
    for start in range(0, slots, CHUNK):
        span = slice(start, start + CHUNK)
        at_src = one_hot_cols(src_col[span], third)
        picked_ref[span, :] = mm(at_src, mid_ref[...]).astype(BF16)
        dst_cols_ref[span, :] = one_hot_cols(dst_col[span], block)
    copies[0].wait()
    for start in range(0, slots, CHUNK):
        span = slice(start, start + CHUNK)
        local = mm(dst_cols_ref[span, :], nodes).astype(BF16)
        dst_pre_ref[span, :] = mm(local, w_dst[...])
    copies[1].wait()
    copies[2].wait()
    top_table = mm(top_own[...], w_top[...]).astype(BF16)
    band_col = column(band_ref[...])
    rows_ref[...] = mm(one_hot_cols(band_col, top_own.shape[0]), top_table)
    for copy in copies[3:]:
        copy.wait()


def first_round(mid, *args):
    top_nodes, cot, w_src = args[0], args[1], args[2]
    slots = args[6].shape[-1]
    block, features = cot.shape
    vmem = pl.BlockSpec(memory_space=pltpu.MemorySpace.VMEM)
    hbm = pltpu.MemorySpace.HBM
    stay = [pltpu.with_memory_space_constraint(array, hbm) for array in args[:6]]
    return pl.pallas_call(
        first_kernel,
        out_shape=(
            jax.ShapeDtypeStruct((slots, features), BF16),
            jax.ShapeDtypeStruct((slots, features), F32),
            jax.ShapeDtypeStruct((block, features), F32),
            jax.ShapeDtypeStruct((slots, block), BF16),
            jax.ShapeDtypeStruct(top_nodes.shape, BF16),
            jax.ShapeDtypeStruct(cot.shape, BF16),
            jax.ShapeDtypeStruct(w_src.shape, BF16),
            jax.ShapeDtypeStruct(w_src.shape, BF16),
        ),
        scratch_shapes=[
            pltpu.VMEM(w_src.shape, BF16),
            pltpu.VMEM(w_src.shape, BF16),
            pltpu.SemaphoreType.DMA((6,)),
        ],
        in_specs=[vmem] + [pl.BlockSpec(memory_space=hbm)] * 6 + [vmem] * 3,
        out_specs=(vmem,) * 8,
        compiler_params=pltpu.CompilerParams(vmem_limit_bytes=32 << 20),
        name="first_round",
    )(mid, *stay, *args[6:])


def block_kernel(
    low_ref,
    mid_ref,
    high_ref,
    src_ref,
    dst_ref,
    band_ref,
    picked_ref,
    dst_pre_ref,
    rows_ref,
    dst_cols,
    top_ref,
    cot_ref,
    w_src,
    w_msg,
    updated_ref,
    grads_ref,
    window_ref,
    ext,
    picked,
    hidden,
    pre_grad,
    act_grad,
    act_slope,
    msg_slope,
):
    slots = src_ref.shape[-1]
    third, features = mid_ref.shape
    block = third // 3
    ext[0:third, :] = low_ref[...]
    ext[third:, :] = high_ref[...]
    nodes = mid_ref[block : 2 * block, :]
    src_row = src_ref[...]
    src_row = jnp.where(src_row < third, src_row, src_row - third)
    inside = (src_ref[...] >= third) & (src_ref[...] < 2 * third)
    src_col = column(jnp.where(inside, -1, src_row))
    dst_rows = one_hot_rows(dst_ref[...], block)
    inflow = rows_ref[...]
    for start in range(0, slots, CHUNK):
        span = slice(start, start + CHUNK)
        other = mm(one_hot_cols(src_col[span], 2 * third), ext[...])
        gathered = (other + picked_ref[span, :].astype(F32)).astype(BF16)
        picked[span, :] = gathered
        pre_act = mm(gathered, w_src[...]) + dst_pre_ref[span, :]
        value, slope = silu_parts(pre_act)
        act_slope[span, :] = slope
        hid = value.astype(BF16)
        hidden[span, :] = hid
        value, slope = silu_parts(mm(hid, w_msg[...]))
        msg_slope[span, :] = slope
        inflow = inflow + mm(dst_rows[:, span], value.astype(BF16))
    value, slope = silu_parts(inflow)
    updated_ref[...] = (nodes.astype(F32) + value).astype(BF16)
    node_grad = (cot_ref[...].astype(F32) * slope).astype(BF16)
    top_nodes = top_ref[...]
    window = mm(one_hot_rows(band_ref[...], top_nodes.shape[0]), node_grad)
    window_ref[...] = window
    grads_ref[3] = mm_rows(top_nodes, window.astype(BF16)).astype(BF16)
    dst_grad = jnp.zeros((block, features), F32)
    for start in range(0, slots, CHUNK):
        span = slice(start, start + CHUNK)
        msg_grad = mm(dst_cols[span, :], node_grad)
        grad = (msg_grad * msg_slope[span, :]).astype(BF16)
        pre_grad[span, :] = grad
        grad = (mm_cols(grad, w_msg[...]) * act_slope[span, :]).astype(BF16)
        act_grad[span, :] = grad
        dst_grad = dst_grad + mm(dst_rows[:, span], grad)
    grads_ref[0] = mm_rows(picked[...], act_grad[...]).astype(BF16)
    grads_ref[1] = mm_rows(nodes, dst_grad.astype(BF16)).astype(BF16)
    grads_ref[2] = mm_rows(hidden[...], pre_grad[...]).astype(BF16)


def block_round(low, mid, high, src_idx, *rest):
    slots = src_idx.shape[-1]
    third, features = mid.shape
    top_rows = rest[6].shape[0]
    vmem = pl.BlockSpec(memory_space=pltpu.MemorySpace.VMEM)
    return pl.pallas_call(
        block_kernel,
        out_shape=(
            jax.ShapeDtypeStruct((third // 3, features), BF16),
            jax.ShapeDtypeStruct((4, features, features), BF16),
            jax.ShapeDtypeStruct((top_rows, features), F32),
        ),
        scratch_shapes=[pltpu.VMEM((2 * third, features), BF16)]
        + [pltpu.VMEM((slots, features), BF16)] * 4
        + [pltpu.VMEM((slots, features), F32)] * 2,
        in_specs=[vmem] * (4 + len(rest)),
        out_specs=(vmem,) * 3,
        compiler_params=pltpu.CompilerParams(vmem_limit_bytes=40 << 20),
        name="block_round",
    )(low, mid, high, src_idx, *rest)


def shards(
    nodes,
    top_nodes,
    cotangent,
    w_src,
    w_dst,
    w_msg,
    w_top,
    src_code,
    src_node,
    dst_node,
    edge_count,
    parent,
):
    block_size, features = nodes.shape[2:]
    slots = src_code.shape[-1]
    top_local = top_nodes.shape[0]
    owner_rows = top_local // lax.axis_size(LON)
    lon_index = lax.axis_index(LON)
    band_start = lax.axis_index(LAT) * top_local
    own = nodes.reshape(block_size, features)
    lat_odd, lon_odd = lax.axis_index("core"), lax.axis_index("x_lo")
    outer = outer_swap(own, LON)
    inner = inner_swap(own, LON)
    mid = jnp.concatenate([outer, own, inner], axis=0)
    low = outer_swap(mid, LAT)
    high = inner_swap(mid, LAT)
    src_row, src_col = src_code // 3, src_code % 3
    src_row = jnp.where(lat_odd == 1, 2 - src_row, src_row)
    src_col = jnp.where(lon_odd == 1, 2 - src_col, src_col)
    src_idx = ((src_row * 3 + src_col) * block_size + src_node).reshape(1, slots)
    live_slot = lax.broadcasted_iota(jnp.int32, (1, slots), 1) < edge_count
    dst_idx = jnp.where(live_slot, dst_node.reshape(1, slots), block_size)
    band_ids = parent.reshape(1, block_size) - band_start
    ready = first_round(
        mid,
        top_nodes,
        cotangent.reshape(block_size, features),
        w_src,
        w_dst,
        w_msg,
        w_top,
        src_idx,
        dst_idx,
        band_ids,
    )
    updated, grads, window = block_round(
        low, mid, high, src_idx, dst_idx, band_ids, *ready
    )
    nodes_total = block_size * lax.axis_size(LAT) * lax.axis_size(LON)
    grad_scale = 8.0 / math.sqrt(nodes_total)
    pairs, near, far = member_groups()
    part = reduce_stage(grads.reshape(-1, features), pairs).astype(BF16)
    part = reduce_stage(part, near).astype(BF16)
    window, part = lax.optimization_barrier((window, lane_tiles(part)))
    padded = jnp.pad(window, ((owner_rows, owner_rows), (0, 0)))
    triple = lax.dynamic_slice_in_dim(padded, lon_index * owner_rows, 3 * owner_rows, 0)
    left, centre, right = jnp.split(triple, 3)
    from_inner = inner_swap(jnp.where(lon_odd == 1, left, right), LON)
    part = (reduce_stage(part, far) * grad_scale).astype(BF16)
    part, from_inner = lax.optimization_barrier((part, from_inner))
    copies, left, right = lax.optimization_barrier((copies_for(part, far), left, right))
    from_outer = outer_swap(jnp.where(lon_odd == 1, right, left), LON)
    table_grad = (centre + from_inner + from_outer).astype(BF16)
    d_top = mm_cols(table_grad, w_top).astype(BF16)
    part = exchange(copies, far)
    part, d_top = lax.optimization_barrier((part, d_top))
    part = gather_stage(whole_rows(part, features), near)
    weight_grads = gather_stage(part, pairs)
    return (
        updated.reshape(nodes.shape),
        weight_grads.reshape(4, features, features),
        d_top,
    )


def solution(mesh):
    lat_count, lon_count = mesh.shape["lat"], mesh.shape["lon"]
    fine = Mesh(
        mesh.devices.reshape(2, lat_count // 8, 2, 2, lon_count // 4, 2, 2),
        AXES,
    )
    placed = (
        P(LAT, LON, None, None),
        P(LAT, None),
        P(LAT, LON, None, None),
        P(),
        P(),
        P(),
        P(),
        P(LAT, LON, None),
        P(LAT, LON, None),
        P(LAT, LON, None),
        P(LAT, LON),
        P(LAT, LON, None),
    )
    return jax.shard_map(
        shards,
        mesh=fine,
        in_specs=placed,
        out_specs=(P(LAT, LON, None, None), P(), P(AXES, None)),
        check_vma=False,
    )
```

```python
import itertools
import math

import jax
import jax.numpy as jnp
from jax import lax
from jax.experimental import pallas as pl
from jax.experimental.pallas import tpu as pltpu
from jax.sharding import Mesh
from jax.sharding import PartitionSpec as P

LAT = ("x_hi", "z_hi", "z_lo", "core")
LON = ("y_hi", "y_lo", "x_lo")
AXES = LAT + LON
LANES = 128
CHUNK = 1024
BF16 = jnp.bfloat16
F32 = jnp.float32


def member_groups():
    sizes = [lax.axis_size(name) for name in AXES]
    groups = ({}, {}, {})
    for device, place in enumerate(itertools.product(*map(range, sizes))):
        at = dict(zip(AXES, place))
        core = at["core"]
        chip = [2 * at[axis + "_hi"] + at[axis + "_lo"] for axis in "xyz"]
        counts = [2 * lax.axis_size(axis + "_hi") for axis in "xyz"]
        moved = [(spot + core) % count for spot, count in zip(chip, counts)]
        cube = tuple(spot // 2 for spot in moved)
        corner = tuple(spot % 2 for spot in moved)
        groups[0].setdefault(tuple(chip), []).append(device)
        groups[1].setdefault((core,) + cube, []).append((corner, device))
        groups[2].setdefault((core,) + corner, []).append((cube, device))
    pairs = list(groups[0].values())
    near, far = ([[device for _, device in sorted(g)] for g in d.values()] for d in groups[1:])
    return pairs, near, far


def exchange(part, groups):
    return lax.all_to_all(part, AXES, 0, 0, axis_index_groups=groups, tiled=True)


def reduce_stage(part, groups):
    got = exchange(part, groups)
    return jnp.sum(got.reshape(len(groups[0]), -1, got.shape[-1]).astype(F32), axis=0)


def gather_stage(part, groups):
    copies = jnp.broadcast_to(part[None], (len(groups[0]),) + part.shape)
    return exchange(copies.reshape(-1, part.shape[-1]), groups)


def lane_tiles(part):
    return jnp.concatenate(jnp.split(part, part.shape[1] // LANES, axis=1), axis=0)


def whole_rows(part, features):
    return jnp.concatenate(jnp.split(part, features // LANES, axis=0), axis=1)


def inner_swap(block, axis):
    count = lax.axis_size(axis)
    return lax.ppermute(block, axis, [(i, i ^ 1) for i in range(count)])


def outer_swap(block, axis):
    count = lax.axis_size(axis)
    partner = {i: i + 1 if i % 2 else i - 1 for i in range(count)}
    return lax.ppermute(block, axis, [(i, j) for i, j in partner.items() if 0 <= j < count])


def silu_parts(values):
    sigmoid_v = jax.nn.sigmoid(values)
    value = values * sigmoid_v
    return value, sigmoid_v + value * (1.0 - sigmoid_v)


def mm(left, right):
    return lax.dot_general(left, right, (((1,), (0,)), ((), ())), preferred_element_type=F32)


def mm_rows(left, right):
    return lax.dot_general(left, right, (((0,), (0,)), ((), ())), preferred_element_type=F32)


def mm_cols(left, right):
    return lax.dot_general(left, right, (((1,), (1,)), ((), ())), preferred_element_type=F32)


def column(row):
    return jnp.transpose(jnp.broadcast_to(row, (8, row.shape[-1])))[:, :1]


def one_hot_cols(ids_column, width):
    lane_ids = lax.broadcasted_iota(jnp.int32, (ids_column.shape[0], width), 1)
    return (ids_column == lane_ids).astype(F32).astype(BF16)


def one_hot_rows(ids_row, height):
    row_ids = lax.broadcasted_iota(jnp.int32, (height, ids_row.shape[-1]), 0)
    return (ids_row == row_ids).astype(F32).astype(BF16)


def first_kernel(
    mid_ref,
    top_ref,
    cot_ref,
    w_src_ref,
    w_dst_ref,
    w_msg_ref,
    w_top_ref,
    src_ref,
    dst_ref,
    band_ref,
    picked_ref,
    dst_pre_ref,
    rows_ref,
    dst_cols_ref,
    top_own,
    cot_own,
    w_src,
    w_msg,
    w_dst,
    w_top,
    arrived,
):
    moves = (
        (w_dst_ref, w_dst),
        (w_top_ref, w_top),
        (top_ref, top_own),
        (w_src_ref, w_src),
        (w_msg_ref, w_msg),
        (cot_ref, cot_own),
    )
    copies = [
        pltpu.make_async_copy(source, target, arrived.at[place])
        for place, (source, target) in enumerate(moves)
    ]
    for copy in copies:
        copy.start()
    slots = src_ref.shape[-1]
    third = mid_ref.shape[0]
    block = third // 3
    nodes = mid_ref[block : 2 * block, :]
    src_col = column(src_ref[...]) - third
    dst_col = column(dst_ref[...])
    for start in range(0, slots, CHUNK):
        span = slice(start, start + CHUNK)
        at_src = one_hot_cols(src_col[span], third)
        picked_ref[span, :] = mm(at_src, mid_ref[...]).astype(BF16)
        dst_cols_ref[span, :] = one_hot_cols(dst_col[span], block)
    copies[0].wait()
    for start in range(0, slots, CHUNK):
        span = slice(start, start + CHUNK)
        local = mm(dst_cols_ref[span, :], nodes).astype(BF16)
        dst_pre_ref[span, :] = mm(local, w_dst[...])
    copies[1].wait()
    copies[2].wait()
    top_table = mm(top_own[...], w_top[...]).astype(BF16)
    band_col = column(band_ref[...])
    rows_ref[...] = mm(one_hot_cols(band_col, top_own.shape[0]), top_table)
    for copy in copies[3:]:
        copy.wait()


def first_round(mid, *args):
    top_nodes, cot, w_src = args[0], args[1], args[2]
    slots = args[6].shape[-1]
    block, features = cot.shape
    vmem = pl.BlockSpec(memory_space=pltpu.MemorySpace.VMEM)
    hbm = pltpu.MemorySpace.HBM
    stay = [pltpu.with_memory_space_constraint(array, hbm) for array in args[:6]]
    return pl.pallas_call(
        first_kernel,
        out_shape=(
            jax.ShapeDtypeStruct((slots, features), BF16),
            jax.ShapeDtypeStruct((slots, features), F32),
            jax.ShapeDtypeStruct((block, features), F32),
            jax.ShapeDtypeStruct((slots, block), BF16),
            jax.ShapeDtypeStruct(top_nodes.shape, BF16),
            jax.ShapeDtypeStruct(cot.shape, BF16),
            jax.ShapeDtypeStruct(w_src.shape, BF16),
            jax.ShapeDtypeStruct(w_src.shape, BF16),
        ),
        scratch_shapes=[
            pltpu.VMEM(w_src.shape, BF16),
            pltpu.VMEM(w_src.shape, BF16),
            pltpu.SemaphoreType.DMA((6,)),
        ],
        in_specs=[vmem] + [pl.BlockSpec(memory_space=hbm)] * 6 + [vmem] * 3,
        out_specs=(vmem,) * 8,
        compiler_params=pltpu.CompilerParams(vmem_limit_bytes=32 << 20),
        name="first_round",
    )(mid, *stay, *args[6:])


def block_kernel(
    low_ref,
    mid_ref,
    high_ref,
    src_ref,
    dst_ref,
    band_ref,
    picked_ref,
    dst_pre_ref,
    rows_ref,
    dst_cols,
    top_ref,
    cot_ref,
    w_src,
    w_msg,
    updated_ref,
    grads_ref,
    window_ref,
    ext,
    picked,
    hidden,
    pre_grad,
    act_grad,
    act_slope,
    msg_slope,
):
    slots = src_ref.shape[-1]
    third, features = mid_ref.shape
    block = third // 3
    ext[0:third, :] = low_ref[...]
    ext[third:, :] = high_ref[...]
    nodes = mid_ref[block : 2 * block, :]
    src_row = src_ref[...]
    src_row = jnp.where(src_row < third, src_row, src_row - third)
    inside = (src_ref[...] >= third) & (src_ref[...] < 2 * third)
    src_col = column(jnp.where(inside, -1, src_row))
    dst_rows = one_hot_rows(dst_ref[...], block)
    inflow = rows_ref[...]
    for start in range(0, slots, CHUNK):
        span = slice(start, start + CHUNK)
        other = mm(one_hot_cols(src_col[span], 2 * third), ext[...])
        gathered = (other + picked_ref[span, :].astype(F32)).astype(BF16)
        picked[span, :] = gathered
        pre_act = mm(gathered, w_src[...]) + dst_pre_ref[span, :]
        value, slope = silu_parts(pre_act)
        act_slope[span, :] = slope
        hid = value.astype(BF16)
        hidden[span, :] = hid
        value, slope = silu_parts(mm(hid, w_msg[...]))
        msg_slope[span, :] = slope
        inflow = inflow + mm(dst_rows[:, span], value.astype(BF16))
    value, slope = silu_parts(inflow)
    updated_ref[...] = (nodes.astype(F32) + value).astype(BF16)
    node_grad = (cot_ref[...].astype(F32) * slope).astype(BF16)
    top_nodes = top_ref[...]
    window = mm(one_hot_rows(band_ref[...], top_nodes.shape[0]), node_grad)
    window_ref[...] = window
    grads_ref[3] = mm_rows(top_nodes, window.astype(BF16)).astype(BF16)
    dst_grad = jnp.zeros((block, features), F32)
    for start in range(0, slots, CHUNK):
        span = slice(start, start + CHUNK)
        msg_grad = mm(dst_cols[span, :], node_grad)
        grad = (msg_grad * msg_slope[span, :]).astype(BF16)
        pre_grad[span, :] = grad
        grad = (mm_cols(grad, w_msg[...]) * act_slope[span, :]).astype(BF16)
        act_grad[span, :] = grad
        dst_grad = dst_grad + mm(dst_rows[:, span], grad)
    grads_ref[0] = mm_rows(picked[...], act_grad[...]).astype(BF16)
    grads_ref[1] = mm_rows(nodes, dst_grad.astype(BF16)).astype(BF16)
    grads_ref[2] = mm_rows(hidden[...], pre_grad[...]).astype(BF16)


def block_round(low, mid, high, src_idx, *rest):
    slots = src_idx.shape[-1]
    third, features = mid.shape
    top_rows = rest[6].shape[0]
    vmem = pl.BlockSpec(memory_space=pltpu.MemorySpace.VMEM)
    return pl.pallas_call(
        block_kernel,
        out_shape=(
            jax.ShapeDtypeStruct((third // 3, features), BF16),
            jax.ShapeDtypeStruct((4, features, features), BF16),
            jax.ShapeDtypeStruct((top_rows, features), F32),
        ),
        scratch_shapes=[pltpu.VMEM((2 * third, features), BF16)]
        + [pltpu.VMEM((slots, features), BF16)] * 4
        + [pltpu.VMEM((slots, features), F32)] * 2,
        in_specs=[vmem] * (4 + len(rest)),
        out_specs=(vmem,) * 3,
        compiler_params=pltpu.CompilerParams(vmem_limit_bytes=40 << 20),
        name="block_round",
    )(low, mid, high, src_idx, *rest)


def shards(
    nodes,
    top_nodes,
    cotangent,
    w_src,
    w_dst,
    w_msg,
    w_top,
    src_code,
    src_node,
    dst_node,
    edge_count,
    parent,
):
    block_size, features = nodes.shape[2:]
    slots = src_code.shape[-1]
    top_local = top_nodes.shape[0]
    owner_rows = top_local // lax.axis_size(LON)
    lon_index = lax.axis_index(LON)
    band_start = lax.axis_index(LAT) * top_local
    own = nodes.reshape(block_size, features)
    lat_odd, lon_odd = lax.axis_index("core"), lax.axis_index("x_lo")
    outer = outer_swap(own, LON)
    inner = inner_swap(own, LON)
    mid = jnp.concatenate([outer, own, inner], axis=0)
    low = outer_swap(mid, LAT)
    high = inner_swap(mid, LAT)
    src_row, src_col = src_code // 3, src_code % 3
    src_row = jnp.where(lat_odd == 1, 2 - src_row, src_row)
    src_col = jnp.where(lon_odd == 1, 2 - src_col, src_col)
    src_idx = ((src_row * 3 + src_col) * block_size + src_node).reshape(1, slots)
    live_slot = lax.broadcasted_iota(jnp.int32, (1, slots), 1) < edge_count
    dst_idx = jnp.where(live_slot, dst_node.reshape(1, slots), block_size)
    band_ids = parent.reshape(1, block_size) - band_start
    ready = first_round(
        mid,
        top_nodes,
        cotangent.reshape(block_size, features),
        w_src,
        w_dst,
        w_msg,
        w_top,
        src_idx,
        dst_idx,
        band_ids,
    )
    updated, grads, window = block_round(
        low, mid, high, src_idx, dst_idx, band_ids, *ready
    )
    nodes_total = block_size * lax.axis_size(LAT) * lax.axis_size(LON)
    grad_scale = 8.0 / math.sqrt(nodes_total)
    pairs, near, far = member_groups()
    part = reduce_stage(grads.reshape(-1, features), pairs).astype(BF16)
    part = reduce_stage(part, near).astype(BF16)
    part = (reduce_stage(lane_tiles(part), far) * grad_scale).astype(BF16)
    window, part = lax.optimization_barrier((window, part))
    padded = jnp.pad(window, ((owner_rows, owner_rows), (0, 0)))
    triple = lax.dynamic_slice_in_dim(padded, lon_index * owner_rows, 3 * owner_rows, 0)
    left, centre, right = jnp.split(triple, 3)
    from_inner = inner_swap(jnp.where(lon_odd == 1, left, right), LON)
    from_outer = outer_swap(jnp.where(lon_odd == 1, right, left), LON)
    table_grad = (centre + from_inner + from_outer).astype(BF16)
    d_top = mm_cols(table_grad, w_top).astype(BF16)
    part = gather_stage(part, far)
    part, d_top = lax.optimization_barrier((part, d_top))
    part = gather_stage(whole_rows(part, features), near)
    weight_grads = gather_stage(part, pairs)
    return (
        updated.reshape(nodes.shape),
        weight_grads.reshape(4, features, features),
        d_top,
    )


def solution(mesh):
    lat_count, lon_count = mesh.shape["lat"], mesh.shape["lon"]
    fine = Mesh(
        mesh.devices.reshape(2, lat_count // 8, 2, 2, lon_count // 4, 2, 2),
        AXES,
    )
    placed = (
        P(LAT, LON, None, None),
        P(LAT, None),
        P(LAT, LON, None, None),
        P(),
        P(),
        P(),
        P(),
        P(LAT, LON, None),
        P(LAT, LON, None),
        P(LAT, LON, None),
        P(LAT, LON),
        P(LAT, LON, None),
    )
    return jax.shard_map(
        shards,
        mesh=fine,
        in_specs=placed,
        out_specs=(P(LAT, LON, None, None), P(), P(AXES, None)),
        check_vma=False,
    )
```

```python
import itertools
import math

import jax
import jax.numpy as jnp
from jax import lax
from jax.experimental import pallas as pl
from jax.experimental.pallas import tpu as pltpu
from jax.sharding import Mesh
from jax.sharding import PartitionSpec as P

LAT = ("x_hi", "z_hi", "z_lo", "core")
LON = ("y_hi", "y_lo", "x_lo")
AXES = LAT + LON
LANES = 128
CHUNK = 512
BF16 = jnp.bfloat16
F32 = jnp.float32


def member_groups():
    sizes = [lax.axis_size(name) for name in AXES]
    groups = ({}, {}, {})
    for device, place in enumerate(itertools.product(*map(range, sizes))):
        at = dict(zip(AXES, place))
        core = at["core"]
        chip = [2 * at[axis + "_hi"] + at[axis + "_lo"] for axis in "xyz"]
        counts = [2 * lax.axis_size(axis + "_hi") for axis in "xyz"]
        moved = [(spot + core) % count for spot, count in zip(chip, counts)]
        cube = tuple(spot // 2 for spot in moved)
        corner = tuple(spot % 2 for spot in moved)
        groups[0].setdefault(tuple(chip), []).append(device)
        groups[1].setdefault((core,) + cube, []).append((corner, device))
        groups[2].setdefault((core,) + corner, []).append((cube, device))
    pairs = list(groups[0].values())
    near, far = ([[device for _, device in sorted(g)] for g in d.values()] for d in groups[1:])
    return pairs, near, far


def exchange(part, groups):
    return lax.all_to_all(part, AXES, 0, 0, axis_index_groups=groups, tiled=True)


def reduce_stage(part, groups):
    got = exchange(part, groups)
    return jnp.sum(got.reshape(len(groups[0]), -1, got.shape[-1]).astype(F32), axis=0)


def gather_stage(part, groups):
    copies = jnp.broadcast_to(part[None], (len(groups[0]),) + part.shape)
    return exchange(copies.reshape(-1, part.shape[-1]), groups)


def lane_tiles(part):
    return jnp.concatenate(jnp.split(part, part.shape[1] // LANES, axis=1), axis=0)


def whole_rows(part, features):
    return jnp.concatenate(jnp.split(part, features // LANES, axis=0), axis=1)


def inner_swap(block, axis):
    count = lax.axis_size(axis)
    return lax.ppermute(block, axis, [(i, i ^ 1) for i in range(count)])


def outer_swap(block, axis):
    count = lax.axis_size(axis)
    partner = {i: i + 1 if i % 2 else i - 1 for i in range(count)}
    return lax.ppermute(block, axis, [(i, j) for i, j in partner.items() if 0 <= j < count])


def silu_parts(values):
    sigmoid_v = jax.nn.sigmoid(values)
    value = values * sigmoid_v
    return value, sigmoid_v + value * (1.0 - sigmoid_v)


def mm(left, right):
    return lax.dot_general(left, right, (((1,), (0,)), ((), ())), preferred_element_type=F32)


def mm_rows(left, right):
    return lax.dot_general(left, right, (((0,), (0,)), ((), ())), preferred_element_type=F32)


def mm_cols(left, right):
    return lax.dot_general(left, right, (((1,), (1,)), ((), ())), preferred_element_type=F32)


def column(row):
    return jnp.transpose(jnp.broadcast_to(row, (8, row.shape[-1])))[:, :1]


def one_hot_cols(ids_column, width):
    lane_ids = lax.broadcasted_iota(jnp.int32, (ids_column.shape[0], width), 1)
    return (ids_column == lane_ids).astype(F32).astype(BF16)


def one_hot_rows(ids_row, height):
    row_ids = lax.broadcasted_iota(jnp.int32, (height, ids_row.shape[-1]), 0)
    return (ids_row == row_ids).astype(F32).astype(BF16)


def first_kernel(
    mid_ref,
    top_ref,
    cot_ref,
    w_src_ref,
    w_dst_ref,
    w_msg_ref,
    w_top_ref,
    src_ref,
    dst_ref,
    band_ref,
    picked_ref,
    dst_pre_ref,
    rows_ref,
    dst_cols_ref,
    top_own,
    cot_own,
    w_src,
    w_msg,
    w_dst,
    w_top,
    arrived,
):
    moves = (
        (w_dst_ref, w_dst),
        (w_top_ref, w_top),
        (top_ref, top_own),
        (w_src_ref, w_src),
        (w_msg_ref, w_msg),
        (cot_ref, cot_own),
    )
    copies = [
        pltpu.make_async_copy(source, target, arrived.at[place])
        for place, (source, target) in enumerate(moves)
    ]
    for copy in copies:
        copy.start()
    slots = src_ref.shape[-1]
    third = mid_ref.shape[0]
    block = third // 3
    nodes = mid_ref[block : 2 * block, :]
    src_col = column(src_ref[...]) - third
    dst_col = column(dst_ref[...])
    for start in range(0, slots, CHUNK):
        span = slice(start, start + CHUNK)
        at_src = one_hot_cols(src_col[span], third)
        picked_ref[span, :] = mm(at_src, mid_ref[...]).astype(BF16)
        dst_cols_ref[span, :] = one_hot_cols(dst_col[span], block)
    copies[0].wait()
    for start in range(0, slots, CHUNK):
        span = slice(start, start + CHUNK)
        local = mm(dst_cols_ref[span, :], nodes).astype(BF16)
        dst_pre_ref[span, :] = mm(local, w_dst[...])
    copies[1].wait()
    copies[2].wait()
    top_table = mm(top_own[...], w_top[...]).astype(BF16)
    band_col = column(band_ref[...])
    rows_ref[...] = mm(one_hot_cols(band_col, top_own.shape[0]), top_table)
    for copy in copies[3:]:
        copy.wait()


def first_round(mid, *args):
    top_nodes, cot, w_src = args[0], args[1], args[2]
    slots = args[6].shape[-1]
    block, features = cot.shape
    vmem = pl.BlockSpec(memory_space=pltpu.MemorySpace.VMEM)
    hbm = pltpu.MemorySpace.HBM
    stay = [pltpu.with_memory_space_constraint(array, hbm) for array in args[:6]]
    return pl.pallas_call(
        first_kernel,
        out_shape=(
            jax.ShapeDtypeStruct((slots, features), BF16),
            jax.ShapeDtypeStruct((slots, features), F32),
            jax.ShapeDtypeStruct((block, features), F32),
            jax.ShapeDtypeStruct((slots, block), BF16),
            jax.ShapeDtypeStruct(top_nodes.shape, BF16),
            jax.ShapeDtypeStruct(cot.shape, BF16),
            jax.ShapeDtypeStruct(w_src.shape, BF16),
            jax.ShapeDtypeStruct(w_src.shape, BF16),
        ),
        scratch_shapes=[
            pltpu.VMEM(w_src.shape, BF16),
            pltpu.VMEM(w_src.shape, BF16),
            pltpu.SemaphoreType.DMA((6,)),
        ],
        in_specs=[vmem] + [pl.BlockSpec(memory_space=hbm)] * 6 + [vmem] * 3,
        out_specs=(vmem,) * 8,
        compiler_params=pltpu.CompilerParams(vmem_limit_bytes=32 << 20),
        name="first_round",
    )(mid, *stay, *args[6:])


def block_kernel(
    low_ref,
    mid_ref,
    high_ref,
    src_ref,
    dst_ref,
    band_ref,
    picked_ref,
    dst_pre_ref,
    rows_ref,
    dst_cols,
    top_ref,
    cot_ref,
    w_src,
    w_msg,
    updated_ref,
    grads_ref,
    window_ref,
    ext,
    picked,
    hidden,
    pre_grad,
    act_grad,
    act_slope,
    msg_slope,
):
    slots = src_ref.shape[-1]
    third, features = mid_ref.shape
    block = third // 3
    ext[0:third, :] = low_ref[...]
    ext[third:, :] = high_ref[...]
    nodes = mid_ref[block : 2 * block, :]
    src_row = src_ref[...]
    src_row = jnp.where(src_row < third, src_row, src_row - third)
    inside = (src_ref[...] >= third) & (src_ref[...] < 2 * third)
    src_col = column(jnp.where(inside, -1, src_row))
    dst_rows = one_hot_rows(dst_ref[...], block)
    inflow = rows_ref[...]
    for start in range(0, slots, CHUNK):
        span = slice(start, start + CHUNK)
        other = mm(one_hot_cols(src_col[span], 2 * third), ext[...])
        gathered = (other + picked_ref[span, :].astype(F32)).astype(BF16)
        picked[span, :] = gathered
        pre_act = mm(gathered, w_src[...]) + dst_pre_ref[span, :]
        value, slope = silu_parts(pre_act)
        act_slope[span, :] = slope
        hid = value.astype(BF16)
        hidden[span, :] = hid
        value, slope = silu_parts(mm(hid, w_msg[...]))
        msg_slope[span, :] = slope
        inflow = inflow + mm(dst_rows[:, span], value.astype(BF16))
    value, slope = silu_parts(inflow)
    updated_ref[...] = (nodes.astype(F32) + value).astype(BF16)
    node_grad = (cot_ref[...].astype(F32) * slope).astype(BF16)
    top_nodes = top_ref[...]
    window = mm(one_hot_rows(band_ref[...], top_nodes.shape[0]), node_grad)
    window_ref[...] = window
    grads_ref[3] = mm_rows(top_nodes, window.astype(BF16)).astype(BF16)
    dst_grad = jnp.zeros((block, features), F32)
    for start in range(0, slots, CHUNK):
        span = slice(start, start + CHUNK)
        msg_grad = mm(dst_cols[span, :], node_grad)
        grad = (msg_grad * msg_slope[span, :]).astype(BF16)
        pre_grad[span, :] = grad
        grad = (mm_cols(grad, w_msg[...]) * act_slope[span, :]).astype(BF16)
        act_grad[span, :] = grad
        dst_grad = dst_grad + mm(dst_rows[:, span], grad)
    grads_ref[0] = mm_rows(picked[...], act_grad[...]).astype(BF16)
    grads_ref[1] = mm_rows(nodes, dst_grad.astype(BF16)).astype(BF16)
    grads_ref[2] = mm_rows(hidden[...], pre_grad[...]).astype(BF16)


def block_round(low, mid, high, src_idx, *rest):
    slots = src_idx.shape[-1]
    third, features = mid.shape
    top_rows = rest[6].shape[0]
    vmem = pl.BlockSpec(memory_space=pltpu.MemorySpace.VMEM)
    return pl.pallas_call(
        block_kernel,
        out_shape=(
            jax.ShapeDtypeStruct((third // 3, features), BF16),
            jax.ShapeDtypeStruct((4, features, features), BF16),
            jax.ShapeDtypeStruct((top_rows, features), F32),
        ),
        scratch_shapes=[pltpu.VMEM((2 * third, features), BF16)]
        + [pltpu.VMEM((slots, features), BF16)] * 4
        + [pltpu.VMEM((slots, features), F32)] * 2,
        in_specs=[vmem] * (4 + len(rest)),
        out_specs=(vmem,) * 3,
        compiler_params=pltpu.CompilerParams(vmem_limit_bytes=40 << 20),
        name="block_round",
    )(low, mid, high, src_idx, *rest)


def shards(
    nodes,
    top_nodes,
    cotangent,
    w_src,
    w_dst,
    w_msg,
    w_top,
    src_code,
    src_node,
    dst_node,
    edge_count,
    parent,
):
    block_size, features = nodes.shape[2:]
    slots = src_code.shape[-1]
    top_local = top_nodes.shape[0]
    owner_rows = top_local // lax.axis_size(LON)
    lon_index = lax.axis_index(LON)
    band_start = lax.axis_index(LAT) * top_local
    own = nodes.reshape(block_size, features)
    lat_odd, lon_odd = lax.axis_index("core"), lax.axis_index("x_lo")
    outer = outer_swap(own, LON)
    inner = inner_swap(own, LON)
    mid = jnp.concatenate([outer, own, inner], axis=0)
    low = outer_swap(mid, LAT)
    high = inner_swap(mid, LAT)
    src_row, src_col = src_code // 3, src_code % 3
    src_row = jnp.where(lat_odd == 1, 2 - src_row, src_row)
    src_col = jnp.where(lon_odd == 1, 2 - src_col, src_col)
    src_idx = ((src_row * 3 + src_col) * block_size + src_node).reshape(1, slots)
    live_slot = lax.broadcasted_iota(jnp.int32, (1, slots), 1) < edge_count
    dst_idx = jnp.where(live_slot, dst_node.reshape(1, slots), block_size)
    band_ids = parent.reshape(1, block_size) - band_start
    ready = first_round(
        mid,
        top_nodes,
        cotangent.reshape(block_size, features),
        w_src,
        w_dst,
        w_msg,
        w_top,
        src_idx,
        dst_idx,
        band_ids,
    )
    updated, grads, window = block_round(
        low, mid, high, src_idx, dst_idx, band_ids, *ready
    )
    nodes_total = block_size * lax.axis_size(LAT) * lax.axis_size(LON)
    grad_scale = 8.0 / math.sqrt(nodes_total)
    first_row = lon_index * owner_rows
    grads, first_row = lax.optimization_barrier((grads, first_row))
    pairs, near, far = member_groups()
    part = reduce_stage(grads.reshape(-1, features), pairs).astype(BF16)
    part = reduce_stage(part, near).astype(BF16)
    part = (reduce_stage(lane_tiles(part), far) * grad_scale).astype(BF16)
    window, part = lax.optimization_barrier((window, part))
    padded = jnp.pad(window, ((owner_rows, owner_rows), (0, 0)))
    triple = lax.dynamic_slice_in_dim(
        padded, first_row, 3 * owner_rows, 0, allow_negative_indices=False
    )
    left, centre, right = jnp.split(triple, 3)
    from_inner = inner_swap(jnp.where(lon_odd == 1, left, right), LON)
    from_outer = outer_swap(jnp.where(lon_odd == 1, right, left), LON)
    table_grad = (centre + from_inner + from_outer).astype(BF16)
    d_top = mm_cols(table_grad, w_top).astype(BF16)
    part = gather_stage(part, far)
    part, d_top = lax.optimization_barrier((part, d_top))
    part = gather_stage(whole_rows(part, features), near)
    weight_grads = gather_stage(part, pairs)
    return (
        updated.reshape(nodes.shape),
        weight_grads.reshape(4, features, features),
        d_top,
    )


def solution(mesh):
    lat_count, lon_count = mesh.shape["lat"], mesh.shape["lon"]
    fine = Mesh(
        mesh.devices.reshape(2, lat_count // 8, 2, 2, lon_count // 4, 2, 2),
        AXES,
    )
    placed = (
        P(LAT, LON, None, None),
        P(LAT, None),
        P(LAT, LON, None, None),
        P(),
        P(),
        P(),
        P(),
        P(LAT, LON, None),
        P(LAT, LON, None),
        P(LAT, LON, None),
        P(LAT, LON),
        P(LAT, LON, None),
    )
    return jax.shard_map(
        shards,
        mesh=fine,
        in_specs=placed,
        out_specs=(P(LAT, LON, None, None), P(), P(AXES, None)),
        check_vma=False,
    )
```

```python
import itertools
import math

import jax
import jax.numpy as jnp
from jax import lax
from jax.experimental import pallas as pl
from jax.experimental.pallas import tpu as pltpu
from jax.sharding import Mesh
from jax.sharding import PartitionSpec as P

LAT = ("x_hi", "z_hi", "z_lo", "core")
LON = ("y_hi", "y_lo", "x_lo")
AXES = LAT + LON
LANES = 128
CHUNK = 512
BF16 = jnp.bfloat16
F32 = jnp.float32


def member_groups():
    sizes = [lax.axis_size(name) for name in AXES]
    groups = ({}, {}, {})
    for device, place in enumerate(itertools.product(*map(range, sizes))):
        at = dict(zip(AXES, place))
        core = at["core"]
        chip = [2 * at[axis + "_hi"] + at[axis + "_lo"] for axis in "xyz"]
        counts = [2 * lax.axis_size(axis + "_hi") for axis in "xyz"]
        moved = [(spot + core) % count for spot, count in zip(chip, counts)]
        cube = tuple(spot // 2 for spot in moved)
        corner = tuple(spot % 2 for spot in moved)
        groups[0].setdefault(tuple(chip), []).append(device)
        groups[1].setdefault((core,) + cube, []).append((corner, device))
        groups[2].setdefault((core,) + corner, []).append((cube, device))
    pairs = list(groups[0].values())
    near, far = ([[device for _, device in sorted(g)] for g in d.values()] for d in groups[1:])
    return pairs, near, far


def exchange(part, groups):
    return lax.all_to_all(part, AXES, 0, 0, axis_index_groups=groups, tiled=True)


def reduce_stage(part, groups):
    got = exchange(part, groups)
    return jnp.sum(got.reshape(len(groups[0]), -1, got.shape[-1]).astype(F32), axis=0)


def gather_stage(part, groups):
    copies = jnp.broadcast_to(part[None], (len(groups[0]),) + part.shape)
    return exchange(copies.reshape(-1, part.shape[-1]), groups)


def lane_tiles(part):
    return jnp.concatenate(jnp.split(part, part.shape[1] // LANES, axis=1), axis=0)


def whole_rows(part, features):
    return jnp.concatenate(jnp.split(part, features // LANES, axis=0), axis=1)


def inner_swap(block, axis):
    count = lax.axis_size(axis)
    return lax.ppermute(block, axis, [(i, i ^ 1) for i in range(count)])


def outer_swap(block, axis):
    count = lax.axis_size(axis)
    partner = {i: i + 1 if i % 2 else i - 1 for i in range(count)}
    return lax.ppermute(block, axis, [(i, j) for i, j in partner.items() if 0 <= j < count])


def silu_parts(values):
    sigmoid_v = jax.nn.sigmoid(values)
    value = values * sigmoid_v
    return value, sigmoid_v + value * (1.0 - sigmoid_v)


def mm(left, right):
    return lax.dot_general(left, right, (((1,), (0,)), ((), ())), preferred_element_type=F32)


def mm_rows(left, right):
    return lax.dot_general(left, right, (((0,), (0,)), ((), ())), preferred_element_type=F32)


def mm_cols(left, right):
    return lax.dot_general(left, right, (((1,), (1,)), ((), ())), preferred_element_type=F32)


def column(row):
    return jnp.transpose(jnp.broadcast_to(row, (8, row.shape[-1])))[:, :1]


def one_hot_cols(ids_column, width):
    lane_ids = lax.broadcasted_iota(jnp.int32, (ids_column.shape[0], width), 1)
    return (ids_column == lane_ids).astype(F32).astype(BF16)


def one_hot_rows(ids_row, height):
    row_ids = lax.broadcasted_iota(jnp.int32, (height, ids_row.shape[-1]), 0)
    return (ids_row == row_ids).astype(F32).astype(BF16)


def first_kernel(
    mid_ref,
    top_ref,
    cot_ref,
    w_src_ref,
    w_dst_ref,
    w_msg_ref,
    w_top_ref,
    src_ref,
    dst_ref,
    band_ref,
    picked_ref,
    dst_pre_ref,
    rows_ref,
    dst_cols_ref,
    top_own,
    cot_own,
    w_src,
    w_msg,
    w_dst,
    w_top,
    arrived,
):
    moves = (
        (w_dst_ref, w_dst),
        (w_top_ref, w_top),
        (top_ref, top_own),
        (w_src_ref, w_src),
        (w_msg_ref, w_msg),
        (cot_ref, cot_own),
    )
    copies = [
        pltpu.make_async_copy(source, target, arrived.at[place])
        for place, (source, target) in enumerate(moves)
    ]
    for copy in copies:
        copy.start()
    slots = src_ref.shape[-1]
    third = mid_ref.shape[0]
    block = third // 3
    nodes = mid_ref[block : 2 * block, :]
    src_col = column(src_ref[...]) - third
    dst_col = column(dst_ref[...])
    for start in range(0, slots, CHUNK):
        span = slice(start, start + CHUNK)
        at_src = one_hot_cols(src_col[span], third)
        picked_ref[span, :] = mm(at_src, mid_ref[...]).astype(BF16)
        dst_cols_ref[span, :] = one_hot_cols(dst_col[span], block)
    copies[0].wait()
    for start in range(0, slots, CHUNK):
        span = slice(start, start + CHUNK)
        local = mm(dst_cols_ref[span, :], nodes).astype(BF16)
        dst_pre_ref[span, :] = mm(local, w_dst[...])
    copies[1].wait()
    copies[2].wait()
    top_table = mm(top_own[...], w_top[...]).astype(BF16)
    band_col = column(band_ref[...])
    rows_ref[...] = mm(one_hot_cols(band_col, top_own.shape[0]), top_table)
    for copy in copies[3:]:
        copy.wait()


def first_round(mid, *args):
    top_nodes, cot, w_src = args[0], args[1], args[2]
    slots = args[6].shape[-1]
    block, features = cot.shape
    vmem = pl.BlockSpec(memory_space=pltpu.MemorySpace.VMEM)
    hbm = pltpu.MemorySpace.HBM
    stay = [pltpu.with_memory_space_constraint(array, hbm) for array in args[:6]]
    return pl.pallas_call(
        first_kernel,
        out_shape=(
            jax.ShapeDtypeStruct((slots, features), BF16),
            jax.ShapeDtypeStruct((slots, features), F32),
            jax.ShapeDtypeStruct((block, features), F32),
            jax.ShapeDtypeStruct((slots, block), BF16),
            jax.ShapeDtypeStruct(top_nodes.shape, BF16),
            jax.ShapeDtypeStruct(cot.shape, BF16),
            jax.ShapeDtypeStruct(w_src.shape, BF16),
            jax.ShapeDtypeStruct(w_src.shape, BF16),
        ),
        scratch_shapes=[
            pltpu.VMEM(w_src.shape, BF16),
            pltpu.VMEM(w_src.shape, BF16),
            pltpu.SemaphoreType.DMA((6,)),
        ],
        in_specs=[vmem] + [pl.BlockSpec(memory_space=hbm)] * 6 + [vmem] * 3,
        out_specs=(vmem,) * 8,
        compiler_params=pltpu.CompilerParams(vmem_limit_bytes=32 << 20),
        name="first_round",
    )(mid, *stay, *args[6:])


def block_kernel(
    low_ref,
    mid_ref,
    high_ref,
    src_ref,
    dst_ref,
    band_ref,
    picked_ref,
    dst_pre_ref,
    rows_ref,
    dst_cols,
    top_ref,
    cot_ref,
    w_src,
    w_msg,
    updated_ref,
    grads_ref,
    window_ref,
    ext,
    picked,
    hidden,
    pre_grad,
    act_grad,
    act_slope,
    msg_slope,
):
    slots = src_ref.shape[-1]
    third, features = mid_ref.shape
    block = third // 3
    ext[0:third, :] = low_ref[...]
    ext[third:, :] = high_ref[...]
    nodes = mid_ref[block : 2 * block, :]
    src_row = src_ref[...]
    src_row = jnp.where(src_row < third, src_row, src_row - third)
    inside = (src_ref[...] >= third) & (src_ref[...] < 2 * third)
    src_col = column(jnp.where(inside, -1, src_row))
    dst_rows = one_hot_rows(dst_ref[...], block)
    inflow = rows_ref[...]
    for start in range(0, slots, CHUNK):
        span = slice(start, start + CHUNK)
        other = mm(one_hot_cols(src_col[span], 2 * third), ext[...])
        gathered = (other + picked_ref[span, :].astype(F32)).astype(BF16)
        picked[span, :] = gathered
        pre_act = mm(gathered, w_src[...]) + dst_pre_ref[span, :]
        value, slope = silu_parts(pre_act)
        act_slope[span, :] = slope
        hid = value.astype(BF16)
        hidden[span, :] = hid
        value, slope = silu_parts(mm(hid, w_msg[...]))
        msg_slope[span, :] = slope
        inflow = inflow + mm(dst_rows[:, span], value.astype(BF16))
    value, slope = silu_parts(inflow)
    updated_ref[...] = (nodes.astype(F32) + value).astype(BF16)
    node_grad = (cot_ref[...].astype(F32) * slope).astype(BF16)
    top_nodes = top_ref[...]
    window = mm(one_hot_rows(band_ref[...], top_nodes.shape[0]), node_grad)
    window_ref[...] = window
    grads_ref[3] = mm_rows(top_nodes, window.astype(BF16)).astype(BF16)
    dst_grad = jnp.zeros((block, features), F32)
    for start in range(0, slots, CHUNK):
        span = slice(start, start + CHUNK)
        msg_grad = mm(dst_cols[span, :], node_grad)
        grad = (msg_grad * msg_slope[span, :]).astype(BF16)
        pre_grad[span, :] = grad
        grad = (mm_cols(grad, w_msg[...]) * act_slope[span, :]).astype(BF16)
        act_grad[span, :] = grad
        dst_grad = dst_grad + mm(dst_rows[:, span], grad)
    grads_ref[0] = mm_rows(picked[...], act_grad[...]).astype(BF16)
    grads_ref[1] = mm_rows(nodes, dst_grad.astype(BF16)).astype(BF16)
    grads_ref[2] = mm_rows(hidden[...], pre_grad[...]).astype(BF16)


def block_round(low, mid, high, src_idx, *rest):
    slots = src_idx.shape[-1]
    third, features = mid.shape
    top_rows = rest[6].shape[0]
    vmem = pl.BlockSpec(memory_space=pltpu.MemorySpace.VMEM)
    return pl.pallas_call(
        block_kernel,
        out_shape=(
            jax.ShapeDtypeStruct((third // 3, features), BF16),
            jax.ShapeDtypeStruct((4, features, features), BF16),
            jax.ShapeDtypeStruct((top_rows, features), F32),
        ),
        scratch_shapes=[pltpu.VMEM((2 * third, features), BF16)]
        + [pltpu.VMEM((slots, features), BF16)] * 4
        + [pltpu.VMEM((slots, features), F32)] * 2,
        in_specs=[vmem] * (4 + len(rest)),
        out_specs=(vmem,) * 3,
        compiler_params=pltpu.CompilerParams(vmem_limit_bytes=40 << 20),
        name="block_round",
    )(low, mid, high, src_idx, *rest)


def shards(
    nodes,
    top_nodes,
    cotangent,
    w_src,
    w_dst,
    w_msg,
    w_top,
    src_code,
    src_node,
    dst_node,
    edge_count,
    parent,
):
    block_size, features = nodes.shape[2:]
    slots = src_code.shape[-1]
    top_local = top_nodes.shape[0]
    owner_rows = top_local // lax.axis_size(LON)
    lon_index = lax.axis_index(LON)
    band_start = lax.axis_index(LAT) * top_local
    own = nodes.reshape(block_size, features)
    lat_odd, lon_odd = lax.axis_index("core"), lax.axis_index("x_lo")
    outer = outer_swap(own, LON)
    inner = inner_swap(own, LON)
    mid = jnp.concatenate([outer, own, inner], axis=0)
    low = outer_swap(mid, LAT)
    high = inner_swap(mid, LAT)
    src_row, src_col = src_code // 3, src_code % 3
    src_row = jnp.where(lat_odd == 1, 2 - src_row, src_row)
    src_col = jnp.where(lon_odd == 1, 2 - src_col, src_col)
    src_idx = ((src_row * 3 + src_col) * block_size + src_node).reshape(1, slots)
    live_slot = lax.broadcasted_iota(jnp.int32, (1, slots), 1) < edge_count
    dst_idx = jnp.where(live_slot, dst_node.reshape(1, slots), block_size)
    band_ids = parent.reshape(1, block_size) - band_start
    ready = first_round(
        mid,
        top_nodes,
        cotangent.reshape(block_size, features),
        w_src,
        w_dst,
        w_msg,
        w_top,
        src_idx,
        dst_idx,
        band_ids,
    )
    updated, grads, window = block_round(
        low, mid, high, src_idx, dst_idx, band_ids, *ready
    )
    nodes_total = block_size * lax.axis_size(LAT) * lax.axis_size(LON)
    grad_scale = 8.0 / math.sqrt(nodes_total)
    padded = jnp.pad(window, ((owner_rows, owner_rows), (0, 0)))
    triple = lax.dynamic_slice_in_dim(padded, lon_index * owner_rows, 3 * owner_rows, 0)
    grads, triple = lax.optimization_barrier((grads, triple))
    pairs, near, far = member_groups()
    part = reduce_stage(grads.reshape(-1, features), pairs).astype(BF16)
    part = reduce_stage(part, near).astype(BF16)
    part = (reduce_stage(lane_tiles(part), far) * grad_scale).astype(BF16)
    triple, part = lax.optimization_barrier((triple, part))
    left, centre, right = jnp.split(triple, 3)
    from_inner = inner_swap(jnp.where(lon_odd == 1, left, right), LON)
    from_outer = outer_swap(jnp.where(lon_odd == 1, right, left), LON)
    table_grad = (centre + from_inner + from_outer).astype(BF16)
    d_top = mm_cols(table_grad, w_top).astype(BF16)
    part = gather_stage(part, far)
    part, d_top = lax.optimization_barrier((part, d_top))
    part = gather_stage(whole_rows(part, features), near)
    weight_grads = gather_stage(part, pairs)
    return (
        updated.reshape(nodes.shape),
        weight_grads.reshape(4, features, features),
        d_top,
    )


def solution(mesh):
    lat_count, lon_count = mesh.shape["lat"], mesh.shape["lon"]
    fine = Mesh(
        mesh.devices.reshape(2, lat_count // 8, 2, 2, lon_count // 4, 2, 2),
        AXES,
    )
    placed = (
        P(LAT, LON, None, None),
        P(LAT, None),
        P(LAT, LON, None, None),
        P(),
        P(),
        P(),
        P(),
        P(LAT, LON, None),
        P(LAT, LON, None),
        P(LAT, LON, None),
        P(LAT, LON),
        P(LAT, LON, None),
    )
    return jax.shard_map(
        shards,
        mesh=fine,
        in_specs=placed,
        out_specs=(P(LAT, LON, None, None), P(), P(AXES, None)),
        check_vma=False,
    )
```
